128 devices in a mesh: img: 16 (over x, y_lo, core), row: 8 (over y_hi, z).
Axes of the slice: x: 4, y: 4 (y_hi: 2, y_lo: 2; y = y_hi * 2 + y_lo), z: 4, core: 2. Of those that a mesh axis runs over, the one named last changes fastest.
Arguments:
- features: bfloat16 [16, 64, 384, 256], P('img', 'row'), may hold values from -6 to 6
- cotangent: bfloat16 [16, 64, 384, 256], P('img', 'row'), may hold values from -6 to 6
- weight_one: bfloat16 [3, 3, 256, 256], replicated, may hold values from -0.125 to 0.125
- weight_two: bfloat16 [3, 3, 256, 256], replicated, may hold values from -0.125 to 0.125
Outputs:
- input_grad: bfloat16 [16, 64, 384, 256], P('img', 'row')
- weight_one_grad: float32 [589824], P(('img', 'row'))
- weight_two_grad: float32 [589824], P(('img', 'row'))
The draws below stay inside these ranges and needn't reach their ends.
All inputs are finite; a program needn't handle non-finite values.
Results may differ from the reference program's by a relative error of at most 0.0055.
Values may be sent and summed in bfloat16 or wider, within the bound.
A program may use at most 128 MiB of HBM per device.

```python
import math
import jax
import jax.numpy as jnp
from jax import lax

C = 256
COLS = 384
HEIGHT = 64
IMAGES = 16


def level_of(own_key, dims, cuts, smallest, top_value):
    def one(dim, parts):
        steps = jax.random.uniform(jax.random.fold_in(jax.random.fold_in(own_key, 6), dim), (parts,), jnp.float32, smallest / len(cuts), top_value / len(cuts))
        return jnp.repeat(jnp.exp(steps), dims[dim] // parts).reshape((-1,) + (1,) * (len(dims) - dim - 1))

    loudness = one(*cuts[0])
    for cut in cuts[1:]:
        loudness = loudness * one(*cut)
    return loudness


def scatter_about(stream_key, shape, spread, reach, split=(), held_as=jnp.bfloat16):
    factor_of = level_of(stream_key, shape, split, -0.22, 0.18) if split else 1.0
    array = jax.random.normal(stream_key, shape, jnp.float32) * spread * factor_of
    return jnp.minimum(jnp.maximum(array, -reach), reach).astype(held_as)


def setup_inputs(seed: int = 0) -> dict:
    arg_keys = jax.random.split(jax.random.key(seed), 5)
    return {
        "features": scatter_about(arg_keys[0], (IMAGES, HEIGHT, COLS, C), 1.0, 6.0, ((0, 16), (1, 8))),
        "cotangent": scatter_about(arg_keys[1], (IMAGES, HEIGHT, COLS, C), 1.0, 6.0, ((0, 16), (1, 8))),
        "weight_one": scatter_about(arg_keys[2], (3, 3, C, C), (9 * C) ** -0.5, 0.125),
        "weight_two": scatter_about(arg_keys[3], (3, 3, C, C), (9 * C) ** -0.5, 0.125),
    }


def gelu_slope(value):
    coeff = 0.7978845608028654
    tanhed = jnp.tanh(coeff * (value + 0.044715 * value * value * value))
    return 0.5 * (1.0 + tanhed) + 0.5 * value * (1.0 - tanhed * tanhed) * coeff * (1.0 + 3.0 * 0.044715 * value * value)

def widen(field):
    return jnp.pad(field, ((0, 0), (1, 1), (0, 0)))

def forward_taps(source, weight):
    rows = source.shape[0] - 2
    cols = source.shape[1]
    chans = source.shape[2]
    padded = widen(source)
    total = jnp.zeros((rows * cols, weight.shape[3]), jnp.float32)
    for tap_row in range(3):
        for tap_col in range(3):
            window = padded[tap_row:tap_row + rows, tap_col:tap_col + cols].reshape(rows * cols, chans)
            total = total + jnp.dot(window, weight[tap_row, tap_col], preferred_element_type=jnp.float32)
    return total.reshape(rows, cols, weight.shape[3])

def backward_taps(source, weight):
    rows = source.shape[0] - 2
    cols = source.shape[1]
    chans = source.shape[2]
    padded = widen(source)
    total = jnp.zeros((rows * cols, weight.shape[2]), jnp.float32)
    for tap_row in range(3):
        for tap_col in range(3):
            window = padded[2 - tap_row:2 - tap_row + rows, 2 - tap_col:2 - tap_col + cols].reshape(rows * cols, chans)
            total = total + lax.dot_general(window, weight[tap_row, tap_col], (((1,), (1,)), ((), ())), preferred_element_type=jnp.float32)
    return total.reshape(rows, cols, weight.shape[2])

def weight_taps(source, grads, offset):
    rows = grads.shape[0]
    cols = grads.shape[1]
    chans = source.shape[2]
    padded = widen(source)
    flat_grads = grads.reshape(rows * cols, grads.shape[2])
    pieces = []
    for tap_row in range(3):
        for tap_col in range(3):
            window = padded[offset + tap_row:offset + tap_row + rows, tap_col:tap_col + cols].reshape(rows * cols, chans)
            pieces.append(lax.dot_general(window, flat_grads, (((0,), (0,)), ((), ())), preferred_element_type=jnp.float32))
    return jnp.stack(pieces)

def local_pass(inputs_wide, grads_wide, inside, weight_one, weight_two):
    rows = inputs_wide.shape[0] - 4
    acted = jax.nn.gelu(inputs_wide.astype(jnp.float32), approximate=True).astype(jnp.bfloat16)
    hidden = forward_taps(acted, weight_one)
    middle = inside[1:rows + 3][:, None, None]
    gated = (jax.nn.gelu(hidden, approximate=True) * middle).astype(jnp.bfloat16)
    back_hidden = backward_taps(grads_wide, weight_two)
    hidden_grad = (back_hidden * gelu_slope(hidden) * middle).astype(jnp.bfloat16)
    back_input = backward_taps(hidden_grad, weight_one)
    own_inputs = inputs_wide[2:rows + 2].astype(jnp.float32)
    own_grads = grads_wide[2:rows + 2]
    input_grad = (own_grads.astype(jnp.float32) + back_input * gelu_slope(own_inputs)).astype(jnp.bfloat16)
    grad_two = weight_taps(gated, own_grads, 0)
    grad_one = weight_taps(acted, hidden_grad[1:rows + 1], 1)
    return (input_grad, grad_one, grad_two)

def reference(features, cotangent, weight_one, weight_two):
    height = features.shape[1]
    chans = features.shape[3]
    places = jnp.arange(height + 4)
    inside = ((places >= 2) & (places < height + 2)).astype(jnp.float32)

    def per_image(carry, pair):
        inputs, grads = pair
        inputs_wide = jnp.pad(inputs, ((2, 2), (0, 0), (0, 0)))
        grads_wide = jnp.pad(grads, ((2, 2), (0, 0), (0, 0)))
        input_grad, grad_one, grad_two = local_pass(inputs_wide, grads_wide, inside, weight_one, weight_two)
        return ((carry[0] + grad_one, carry[1] + grad_two), input_grad)
    empty = jnp.zeros((9, chans, chans), jnp.float32)
    totals, input_grads = lax.scan(per_image, (empty, empty), (features, cotangent))
    scale = 1.0 / math.sqrt(features.shape[0] * height * features.shape[2])
    return (input_grads, (totals[0] * scale).reshape(-1), (totals[1] * scale).reshape(-1))
```

```python
import functools
import math

import jax
import jax.numpy as jnp
from jax import lax
from jax.experimental import pallas as pl
from jax.experimental.pallas import tpu as pltpu
from jax.sharding import PartitionSpec as P

MESH = pl.DeviceIdType.MESH
F32 = jnp.float32
BF16 = jnp.bfloat16
COEFF = 0.7978845608028654
CUBIC = 0.044715
ROWS = 8
COLS = 384
CHANS = 256
WIDE = 3 * CHANS
CELLS = ROWS * COLS
GROUP = 144
PIECE = 18


def gelu_parts(v):
    sq = v * v
    t = jnp.tanh(COEFF * v * (1.0 + CUBIC * sq))
    half = 0.5 * (1.0 + t)
    slope = half + (0.5 * COEFF) * v * (1.0 - t * t) * (1.0 + (3.0 * CUBIC) * sq)
    return v * half, slope


def shifted(v):
    index = lax.broadcasted_iota(jnp.int32, v.shape, 0)
    left = jnp.where(index == 0, 0.0, pltpu.roll(v, 1, 0))
    right = jnp.where(index == COLS - 1, 0.0, pltpu.roll(v, COLS - 1, 0))
    return left, right


def span(row):
    if isinstance(row, int):
        return pl.ds(row * COLS, COLS)
    return pl.ds(pl.multiple_of(row * COLS, COLS), COLS)


def kernel(
    scale,
    feat,
    cot,
    w_one,
    w_two,
    out,
    out_one,
    out_two,
    fv,
    gv,
    wv1,
    wv2,
    wt1,
    wt2,
    a3,
    g3,
    h3,
    at,
    gt,
    slope,
    hid,
    bh,
    hsend,
    hrecv,
    stage,
    acc,
    crecv,
    xsend,
    xrecv,
    xown,
    ysend,
    yrecv,
    yown,
    zsend,
    zrecv,
    zown,
    load_sem,
    w_sem,
    halo_send,
    halo_recv,
    out_sem,
    core_send,
    core_recv,
    ring_send,
    ring_recv,
):
    img, row = lax.axis_index("img"), lax.axis_index("row")
    core, y_lo, x = img % 2, (img // 2) % 2, img // 4
    z, y_hi = row % 4, row // 4
    y = y_hi * 2 + y_lo

    def x_peer(k):
        there = (x + k) % 4
        return there, ((there * 2 + y_lo) * 2 + core, row)

    def y_peer(k):
        there = (y + k) % 4
        return there, ((x * 2 + there % 2) * 2 + core, (there // 2) * 4 + z)

    def z_peer(k):
        there = (z + k) % 4
        return there, (img, y_hi * 4 + there)

    partner = ((x * 2 + y_lo) * 2 + (1 - core), row)
    below, above = (img, (row + 1) % 8), (img, (row + 7) % 8)

    barrier = pltpu.get_barrier_semaphore()
    peers = [partner, below, above]
    for peer in (x_peer, y_peer, z_peer):
        for k in (1, 2, 3):
            peers.append(peer(k)[1])
    for peer in peers:
        pl.semaphore_signal(barrier, inc=1, device_id=peer, device_id_type=MESH)

    loads = [
        pltpu.make_async_copy(feat.at[0, r], fv.at[span(r + 1)], load_sem.at[0, r]) for r in range(ROWS)
    ] + [pltpu.make_async_copy(cot.at[0, r], gv.at[span(r + 1)], load_sem.at[1, r]) for r in range(ROWS)]
    weights = [
        pltpu.make_async_copy(w_one, wv1, w_sem.at[0]),
        pltpu.make_async_copy(w_two, wv2, w_sem.at[1]),
    ]
    for copy in weights + loads:
        copy.start()
    pl.semaphore_wait(barrier, len(peers))

    def halo(which, down, src, dst):
        return pltpu.make_async_remote_copy(
            src_ref=src,
            dst_ref=dst,
            send_sem=halo_send.at[which, down],
            recv_sem=halo_recv.at[which, down],
            device_id=below if down else above,
            device_id_type=MESH,
        )

    halos_down = [
        halo(0, 1, feat.at[0, ROWS - 1], fv.at[span(0)]),
        halo(1, 1, cot.at[0, ROWS - 1], gv.at[span(0)]),
    ]
    halos_up = [
        halo(0, 0, feat.at[0, 0], fv.at[span(ROWS + 1)]),
        halo(1, 0, cot.at[0, 0], gv.at[span(ROWS + 1)]),
    ]
    h_down = halo(2, 1, hsend.at[1], hrecv.at[0])
    h_up = halo(2, 0, hsend.at[0], hrecv.at[1])

    @pl.when(row < 7)
    def _():
        for copy in halos_down:
            copy.start()

    @pl.when(row > 0)
    def _():
        for copy in halos_up:
            copy.start()

    for copy in weights:
        copy.wait()

    def turn(tap, _):
        a, b = tap // 3, tap % 3
        wt1[a, pl.ds(pl.multiple_of(b * CHANS, CHANS), CHANS), :] = wv1[a, b].T
        wt2[a, pl.ds(pl.multiple_of(b * CHANS, CHANS), CHANS), :] = wv2[a, b].T
        return 0

    lax.fori_loop(0, 9, turn, 0)

    def prep(r, own):
        for lane in (0, 128):
            v = fv[span(r), lane : lane + 128].astype(F32)
            acted, grade = gelu_parts(v)
            if own:
                slope[span(r - 1), lane : lane + 128] = grade
            left, right = shifted(acted)
            mid = acted.astype(BF16)
            a3[span(r), lane : lane + 128] = left.astype(BF16)
            a3[span(r), CHANS + lane : CHANS + lane + 128] = mid
            a3[span(r), 2 * CHANS + lane : 2 * CHANS + lane + 128] = right.astype(BF16)
            at[lane : lane + 128, span(r)] = mid.T
            g = gv[span(r), lane : lane + 128]
            left, right = shifted(g.astype(F32))
            g3[span(r), lane : lane + 128] = right.astype(BF16)
            g3[span(r), CHANS + lane : CHANS + lane + 128] = g
            g3[span(r), 2 * CHANS + lane : 2 * CHANS + lane + 128] = left.astype(BF16)

    for copy in loads:
        copy.wait()
    lax.fori_loop(1, ROWS + 1, lambda r, _: (prep(r, True), 0)[1], 0)

    def conv(source, weight, r, flip):
        total = None
        for a in range(3):
            near = r - a + 1 if flip else r + a - 1
            part = jnp.dot(source[span(near), :], weight(a), preferred_element_type=F32)
            total = part if total is None else total + part
        return total

    def forward_one(a):
        return wv1[a].reshape(WIDE, CHANS)

    def widen_grad(r, lane, h):
        left, right = shifted(h)
        h3[span(r), lane : lane + 128] = right.astype(BF16)
        h3[span(r), CHANS + lane : CHANS + lane + 128] = h.astype(BF16)
        h3[span(r), 2 * CHANS + lane : 2 * CHANS + lane + 128] = left.astype(BF16)

    def middle(r):
        hid[...] = conv(a3, forward_one, r, False)
        bh[...] = conv(g3, lambda a: wt2[a], r, True)
        for lane in (0, 128):
            gated, grade = gelu_parts(hid[:, lane : lane + 128])
            gt[lane : lane + 128, span(r - 1)] = gated.astype(BF16).T
            widen_grad(r, lane, bh[:, lane : lane + 128] * grade)

    lax.fori_loop(2, ROWS, lambda r, _: (middle(r), 0)[1], 0)

    @pl.when(row > 0)
    def _():
        for copy in halos_down:
            copy.wait_recv()

    @pl.when(row == 0)
    def _():
        fv[span(0), :] = jnp.zeros((COLS, CHANS), BF16)
        gv[span(0), :] = jnp.zeros((COLS, CHANS), BF16)

    @pl.when(row < 7)
    def _():
        for copy in halos_up:
            copy.wait_recv()

    @pl.when(row == 7)
    def _():
        fv[span(ROWS + 1), :] = jnp.zeros((COLS, CHANS), BF16)
        gv[span(ROWS + 1), :] = jnp.zeros((COLS, CHANS), BF16)

    lax.fori_loop(0, 2, lambda i, _: (prep(i * (ROWS + 1), False), 0)[1], 0)
    lax.fori_loop(0, 2, lambda i, _: (middle(1 + i * (ROWS - 1)), 0)[1], 0)

    hsend[0] = h3[span(1), CHANS : 2 * CHANS]
    hsend[1] = h3[span(ROWS), CHANS : 2 * CHANS]

    @pl.when(row < 7)
    def _():
        h_down.start()

    @pl.when(row > 0)
    def _():
        h_up.start()

    def core_copy(t, g):
        return pltpu.make_async_remote_copy(
            src_ref=acc.at[t, pl.ds(pl.multiple_of((2 * g + 1 - core) * GROUP, GROUP), GROUP)],
            dst_ref=crecv.at[t, g],
            send_sem=core_send.at[t, g],
            recv_sem=core_recv.at[t, g],
            device_id=partner,
            device_id_type=MESH,
        )

    def stage_copy(t, which, k):
        peer = (x_peer, y_peer, z_peer)[which]
        send, recv = ((xsend, xrecv), (ysend, yrecv), (zsend, zrecv))[which]
        there, device = peer(k)
        return pltpu.make_async_remote_copy(
            src_ref=send.at[t, there],
            dst_ref=recv.at[t, k - 1],
            send_sem=ring_send.at[t, which, k - 1],
            recv_sem=ring_recv.at[t, which, k - 1],
            device_id=device,
            device_id_type=MESH,
        )

    def core_start(t):
        for g in range(8):
            core_copy(t, g).start()

    def x_start(t):
        for g in range(8):
            core_copy(t, g).wait_recv()

        def add(g, _):
            here = pl.ds(pl.multiple_of((2 * g + core) * GROUP, GROUP), GROUP)
            total = acc[t, here, :] + crecv[t, g]
            place = pl.ds(pl.multiple_of((g % 2) * GROUP, GROUP), GROUP)
            xsend[t, g // 2, place, :] = total.astype(BF16)

            @pl.when(g // 2 == x)
            def _():
                xown[t, place, :] = total

            return 0

        lax.fori_loop(0, 8, add, 0)
        for k in (2, 1, 3):
            stage_copy(t, 0, k).start()

    def y_start(t):
        for k in (1, 2, 3):
            stage_copy(t, 0, k).wait_recv()
        for part in range(4):
            here = slice((part % 2) * GROUP + (part // 2) * 72, (part % 2) * GROUP + (part // 2) * 72 + 72)
            total = xown[t, here, :]
            for k in range(3):
                total = total + xrecv[t, k, here, :].astype(F32)
            yown[t, part] = total
            ysend[t, part] = total.astype(BF16)
        for k in (2, 1, 3):
            stage_copy(t, 1, k).start()

    def z_start(t):
        for k in (1, 2, 3):
            stage_copy(t, 1, k).wait_recv()
        total = yown[t, y]
        for k in range(3):
            total = total + yrecv[t, k].astype(F32)
        yown[t, y] = total
        for part in range(4):
            piece = yown[t, y, part * PIECE : part * PIECE + PIECE, :]
            zown[t, part] = piece
            zsend[t, part] = piece.astype(BF16)
        for k in (2, 1, 3):
            stage_copy(t, 2, k).start()

    def finish(t, result):
        for k in (1, 2, 3):
            stage_copy(t, 2, k).wait_recv()
        total = zown[t, z]
        for k in range(3):
            total = total + zrecv[t, k].astype(F32)
        result[...] = total * scale

    def grads(t, a):
        if t:
            product = jnp.dot(gt[...], g3[(2 - a) * COLS : (2 - a) * COLS + CELLS, :], preferred_element_type=F32)
        else:
            product = jnp.dot(
                at[:, a * COLS : a * COLS + CELLS], h3[COLS : COLS + CELLS, :], preferred_element_type=F32
            )
        for b in range(3):
            acc[t, (a * 3 + b) * CHANS : (a * 3 + b + 1) * CHANS, :] = product[:, b * CHANS : (b + 1) * CHANS]

    def out_copy(r):
        return pltpu.make_async_copy(stage.at[span(r - 1)], out.at[0, r - 1], out_sem.at[r - 1])

    def last(r):
        total = conv(h3, lambda a: wt1[a], r, True)
        stage[span(r - 1), :] = (
            gv[span(r), :].astype(F32) + total * slope[span(r - 1), :]
        ).astype(BF16)
        out_copy(r).start()

    def last_rows(first, end):
        lax.fori_loop(first, end, lambda r, _: (last(r), 0)[1], 0)

    for a in range(3):
        grads(1, a)
    core_start(1)
    grads(0, 0)
    x_start(1)
    grads(0, 1)
    grads(0, 2)
    core_start(0)
    last_rows(2, 4)
    x_start(0)
    last_rows(4, 6)
    y_start(1)
    last_rows(6, 8)
    z_start(1)

    @pl.when(row > 0)
    def _():
        h_down.wait_recv()

    @pl.when(row == 0)
    def _():
        hrecv[0] = jnp.zeros((COLS, CHANS), BF16)

    @pl.when(row < 7)
    def _():
        h_up.wait_recv()

    @pl.when(row == 7)
    def _():
        hrecv[1] = jnp.zeros((COLS, CHANS), BF16)

    for end in range(2):
        for lane in (0, 128):
            widen_grad(end * (ROWS + 1), lane, hrecv[end, :, lane : lane + 128].astype(F32))
    lax.fori_loop(0, 2, lambda i, _: (last(1 + i * (ROWS - 1)), 0)[1], 0)

    y_start(0)
    finish(1, out_two)
    z_start(0)
    finish(0, out_one)

    @pl.when(row < 7)
    def _():
        for copy in halos_down + [h_down]:
            copy.wait_send()

    @pl.when(row > 0)
    def _():
        for copy in halos_up + [h_up]:
            copy.wait_send()

    for r in range(ROWS):
        out_copy(r + 1).wait()
    for t in range(2):
        for g in range(8):
            core_copy(t, g).wait_send()
        for which in range(3):
            for k in (1, 2, 3):
                stage_copy(t, which, k).wait_send()


def shards(features, cotangent, weight_one, weight_two):
    height = features.shape[1] * lax.axis_size("row")
    scale = 1.0 / math.sqrt(lax.axis_size("img") * height * features.shape[2])
    hbm = pl.BlockSpec(memory_space=pl.ANY)
    vmem = pl.BlockSpec(memory_space=pltpu.VMEM)
    dma = pltpu.SemaphoreType.DMA
    wide_cells = (ROWS + 2) * COLS
    grad, one, two = pl.pallas_call(
        functools.partial(kernel, scale),
        out_shape=(
            jax.ShapeDtypeStruct(features.shape, BF16),
            jax.ShapeDtypeStruct((PIECE, CHANS), F32),
            jax.ShapeDtypeStruct((PIECE, CHANS), F32),
        ),
        in_specs=[hbm] * 4,
        out_specs=(hbm, vmem, vmem),
        scratch_shapes=[
            pltpu.VMEM((wide_cells, CHANS), BF16),
            pltpu.VMEM((wide_cells, CHANS), BF16),
            pltpu.VMEM((3, 3, CHANS, CHANS), BF16),
            pltpu.VMEM((3, 3, CHANS, CHANS), BF16),
            pltpu.VMEM((3, WIDE, CHANS), BF16),
            pltpu.VMEM((3, WIDE, CHANS), BF16),
            pltpu.VMEM((wide_cells, WIDE), BF16),
            pltpu.VMEM((wide_cells, WIDE), BF16),
            pltpu.VMEM((wide_cells, WIDE), BF16),
            pltpu.VMEM((CHANS, wide_cells), BF16),
            pltpu.VMEM((CHANS, CELLS), BF16),
            pltpu.VMEM((CELLS, CHANS), F32),
            pltpu.VMEM((COLS, CHANS), F32),
            pltpu.VMEM((COLS, CHANS), F32),
            pltpu.VMEM((2, COLS, CHANS), BF16),
            pltpu.VMEM((2, COLS, CHANS), BF16),
            pltpu.VMEM((CELLS, CHANS), BF16),
            pltpu.VMEM((2, 9 * CHANS, CHANS), F32),
            pltpu.VMEM((2, 8, GROUP, CHANS), F32),
            pltpu.VMEM((2, 4, 2 * GROUP, CHANS), BF16),
            pltpu.VMEM((2, 3, 2 * GROUP, CHANS), BF16),
            pltpu.VMEM((2, 2 * GROUP, CHANS), F32),
            pltpu.VMEM((2, 4, GROUP // 2, CHANS), BF16),
            pltpu.VMEM((2, 3, GROUP // 2, CHANS), BF16),
            pltpu.VMEM((2, 4, GROUP // 2, CHANS), F32),
            pltpu.VMEM((2, 4, PIECE, CHANS), BF16),
            pltpu.VMEM((2, 3, PIECE, CHANS), BF16),
            pltpu.VMEM((2, 4, PIECE, CHANS), F32),
            dma((2, ROWS)),
            dma((2,)),
            dma((3, 2)),
            dma((3, 2)),
            dma((ROWS,)),
            dma((2, 8)),
            dma((2, 8)),
            dma((2, 3, 3)),
            dma((2, 3, 3)),
        ],
        compiler_params=pltpu.CompilerParams(
            collective_id=0, has_side_effects=True, vmem_limit_bytes=64 * 1000 * 1000
        ),
        name="unit_backward",
    )(features, cotangent, weight_one, weight_two)
    return grad, one.reshape(-1), two.reshape(-1)


def solution(mesh):
    placed = (P("img", "row", None, None), P("img", "row", None, None), P(), P())
    return jax.shard_map(
        shards,
        mesh=mesh,
        in_specs=placed,
        out_specs=(P("img", "row", None, None), P(("img", "row")), P(("img", "row"))),
        check_vma=False,
    )
```

```python
import functools
import math

import jax
import jax.numpy as jnp
from jax import lax
from jax.experimental import pallas as pl
from jax.experimental.pallas import tpu as pltpu
from jax.sharding import PartitionSpec as P

MESH = pl.DeviceIdType.MESH
F32 = jnp.float32
BF16 = jnp.bfloat16
COEFF = 0.7978845608028654
CUBIC = 0.044715
ROWS = 8
COLS = 384
CHANS = 256
WIDE = 3 * CHANS
CELLS = ROWS * COLS
GROUP = 144
PIECE = 18


def gelu_terms(v):
    poly = COEFF + (COEFF * CUBIC) * (v * v)
    half = 0.5 + 0.5 * jnp.tanh(v * poly)
    return v * half, half, poly


def slope_of(acted, half, poly):
    return half + acted * (1.0 - half) * (6.0 * poly - 4.0 * COEFF)


def shifted(v):
    index = lax.broadcasted_iota(jnp.int32, v.shape, 0)
    left = jnp.where(index == 0, 0.0, pltpu.roll(v, 1, 0))
    right = jnp.where(index == COLS - 1, 0.0, pltpu.roll(v, COLS - 1, 0))
    return left, right


def span(row, count=1):
    return slice(row * COLS, (row + count) * COLS)


def kernel(
    scale,
    feat,
    cot,
    w_one,
    w_two,
    out,
    out_one,
    out_two,
    fv,
    gv,
    wv1,
    wv2,
    wt1,
    wt2,
    a3,
    g3,
    h3,
    at,
    gt,
    slope,
    hid,
    bh,
    hsend,
    hrecv,
    stage,
    acc,
    crecv,
    send1,
    recv1,
    own1,
    send2,
    recv2,
    own2,
    send3,
    recv3,
    own3,
    load_sem,
    w_sem,
    halo_send,
    halo_recv,
    out_sem,
    core_send,
    core_recv,
    wide_send,
    wide_recv,
    last_send,
    last_recv,
):
    img, row = lax.axis_index("img"), lax.axis_index("row")
    core, y_lo, x = img % 2, (img // 2) % 2, img // 4
    z, y_hi = row % 4, row // 4
    y = y_hi * 2 + y_lo

    def x_peer(k):
        there = (x + k) % 4
        return there, ((there * 2 + y_lo) * 2 + core, row)

    def y_peer(k):
        there = (y + k) % 4
        return there, ((x * 2 + there % 2) * 2 + core, (there // 2) * 4 + z)

    def z_peer(k):
        there = (z + k) % 4
        return there, (img, y_hi * 4 + there)

    partner = ((x * 2 + y_lo) * 2 + (1 - core), row)
    below, above = (img, (row + 1) % 8), (img, (row + 7) % 8)

    loads = [
        (
            pltpu.make_async_copy(feat.at[0, r], fv.at[span(r + 1)], load_sem.at[0, r]),
            pltpu.make_async_copy(cot.at[0, r], gv.at[span(r + 1)], load_sem.at[1, r]),
        )
        for r in range(ROWS)
    ]
    weights = [
        pltpu.make_async_copy(w_one, wv1, w_sem.at[0]),
        pltpu.make_async_copy(w_two, wv2, w_sem.at[1]),
    ]
    for pair in loads[:4]:
        for copy in pair:
            copy.start()
    for copy in weights:
        copy.start()
    for pair in loads[4:]:
        for copy in pair:
            copy.start()

    barrier = pltpu.get_barrier_semaphore()
    peers = [partner, below, above]
    for peer in (x_peer, y_peer, z_peer):
        for k in (1, 2, 3):
            peers.append(peer(k)[1])
    for peer in peers:
        pl.semaphore_signal(barrier, inc=1, device_id=peer, device_id_type=MESH)
    pl.semaphore_wait(barrier, len(peers))

    def halo(which, down, src, dst):
        return pltpu.make_async_remote_copy(
            src_ref=src,
            dst_ref=dst,
            send_sem=halo_send.at[which, down],
            recv_sem=halo_recv.at[which, down],
            device_id=below if down else above,
            device_id_type=MESH,
        )

    halos_down = [
        halo(0, 1, feat.at[0, ROWS - 1], fv.at[span(0)]),
        halo(1, 1, cot.at[0, ROWS - 1], gv.at[span(0)]),
    ]
    halos_up = [
        halo(0, 0, feat.at[0, 0], fv.at[span(ROWS + 1)]),
        halo(1, 0, cot.at[0, 0], gv.at[span(ROWS + 1)]),
    ]
    h_down = halo(2, 1, hsend.at[1], hrecv.at[0])
    h_up = halo(2, 0, hsend.at[0], hrecv.at[1])

    @pl.when(row < 7)
    def _():
        for copy in halos_down:
            copy.start()

    @pl.when(row > 0)
    def _():
        for copy in halos_up:
            copy.start()

    def turn(source, target):
        for a in range(3):
            for b in range(3):
                target[a, b * CHANS : (b + 1) * CHANS, :] = source[a, b].T

    def prep(r):
        for lane in (0, 128):
            acted, _, _ = gelu_terms(fv[span(r), lane : lane + 128].astype(F32))
            left, right = shifted(acted)
            mid = acted.astype(BF16)
            a3[span(r), lane : lane + 128] = left.astype(BF16)
            a3[span(r), CHANS + lane : CHANS + lane + 128] = mid
            a3[span(r), 2 * CHANS + lane : 2 * CHANS + lane + 128] = right.astype(BF16)
            at[lane : lane + 128, span(r)] = mid.T
            g = gv[span(r), lane : lane + 128]
            left, right = shifted(g.astype(F32))
            g3[span(r), lane : lane + 128] = right.astype(BF16)
            g3[span(r), CHANS + lane : CHANS + lane + 128] = g
            g3[span(r), 2 * CHANS + lane : 2 * CHANS + lane + 128] = left.astype(BF16)

    def grade(r):
        for lane in (0, 128):
            slope[span(r - 1), lane : lane + 128] = slope_of(
                *gelu_terms(fv[span(r), lane : lane + 128].astype(F32))
            )

    def conv(source, weight, r, count, flip):
        total = None
        for a in range(3):
            near = r - a + 1 if flip else r + a - 1
            part = jnp.dot(source[span(near, count), :], weight(a), preferred_element_type=F32)
            total = part if total is None else total + part
        return total

    def forward_one(a):
        return wv1[a].reshape(WIDE, CHANS)

    def convs(r, count, slot):
        hid[slot, : count * COLS, :] = conv(a3, forward_one, r, count, False)
        bh[slot, : count * COLS, :] = conv(g3, lambda a: wt2[a], r, count, True)

    def widen_grad(r, lane, h):
        left, right = shifted(h)
        h3[span(r), lane : lane + 128] = right.astype(BF16)
        h3[span(r), CHANS + lane : CHANS + lane + 128] = h.astype(BF16)
        h3[span(r), 2 * CHANS + lane : 2 * CHANS + lane + 128] = left.astype(BF16)

    def elem(r, slot, part):
        for lane in (0, 128):
            terms = gelu_terms(hid[slot, span(part), lane : lane + 128])
            gt[lane : lane + 128, span(r - 1)] = terms[0].astype(BF16).T
            widen_grad(r, lane, bh[slot, span(part), lane : lane + 128] * slope_of(*terms))

    def grads(t, a, r, count, fresh):
        if t:
            left, right = gt[:, span(r - 1, count)], g3[span(r - a + 1, count), :]
        else:
            left, right = at[:, span(r + a - 1, count)], h3[span(r, count), :]
        product = jnp.dot(left, right, preferred_element_type=F32)
        for b in range(3):
            here = slice((a * 3 + b) * CHANS, (a * 3 + b + 1) * CHANS)
            piece = product[:, b * CHANS : (b + 1) * CHANS]
            acc[t, here, :] = piece if fresh else acc[t, here, :] + piece

    def core_copy(t, g):
        return pltpu.make_async_remote_copy(
            src_ref=acc.at[t, pl.ds(pl.multiple_of((2 * g + 1 - core) * GROUP, GROUP), GROUP)],
            dst_ref=crecv.at[t, g],
            send_sem=core_send.at[t, g],
            recv_sem=core_recv.at[t, g],
            device_id=partner,
            device_id_type=MESH,
        )

    def wide_copy(t, color, step, k):
        send, recv = ((send1, recv1), (send2, recv2))[step]
        there, device = (x_peer if color == step else y_peer)(k)
        return pltpu.make_async_remote_copy(
            src_ref=send.at[t, color, there],
            dst_ref=recv.at[t, color, k - 1],
            send_sem=wide_send.at[t, color, step, k - 1],
            recv_sem=wide_recv.at[t, color, step, k - 1],
            device_id=device,
            device_id_type=MESH,
        )

    def last_copy(t, k):
        there, device = z_peer(k)
        return pltpu.make_async_remote_copy(
            src_ref=send3.at[t, there],
            dst_ref=recv3.at[t, k - 1],
            send_sem=last_send.at[t, k - 1],
            recv_sem=last_recv.at[t, k - 1],
            device_id=device,
            device_id_type=MESH,
        )

    HALF = GROUP // 2
    LEFT, RIGHT = slice(0, 128), slice(128, 256)

    def core_start(t, a):
        for g in ((0, 1), (2, 3, 4), (5, 6, 7))[a]:
            core_copy(t, g).start()

    def core_add(t, a):
        for g in ((0, 1), (2, 3, 4), (5, 6, 7))[a]:
            core_copy(t, g).wait_recv()
            here = pl.ds(pl.multiple_of((2 * g + core) * GROUP, GROUP), GROUP)
            total = acc[t, here, :] + crecv[t, g]
            crecv[t, g] = total
            place, low = g // 2, g % 2
            send1[t, 0, place, low * GROUP : (low + 1) * GROUP, :] = total[:, LEFT].astype(BF16)
            for high in range(2):
                send1[t, 1, high * 2 + low, place * HALF : (place + 1) * HALF, :] = total[
                    high * HALF : (high + 1) * HALF, RIGHT
                ].astype(BF16)

    def start1(t):
        for k in (2, 1, 3):
            for color in range(2):
                wide_copy(t, color, 0, k).start()

    def start2(t):
        for color in range(2):
            for k in (1, 2, 3):
                wide_copy(t, color, 0, k).wait_recv()
        for low in range(2):
            for high in range(2):
                rows = slice(low * GROUP + high * HALF, low * GROUP + (high + 1) * HALF)
                total = crecv[t, 2 * x + low, high * HALF : (high + 1) * HALF, LEFT]
                for k in range(3):
                    total = total + recv1[t, 0, k, rows, :].astype(F32)
                own1[t, 0, high * 2 + low] = total
                send2[t, 0, high * 2 + low] = total.astype(BF16)
        for place in range(4):
            rows = slice(place * HALF, (place + 1) * HALF)
            total = crecv[t, 2 * place + y_lo, pl.ds(pl.multiple_of(y_hi * HALF, HALF), HALF), RIGHT]
            for k in range(3):
                total = total + recv1[t, 1, k, rows, :].astype(F32)
            own1[t, 1, place] = total
            send2[t, 1, place] = total.astype(BF16)
        for k in (2, 1, 3):
            for color in range(2):
                wide_copy(t, color, 1, k).start()

    def start3(t):
        for color, mine in ((0, y), (1, x)):
            for k in (1, 2, 3):
                wide_copy(t, color, 1, k).wait_recv()
            total = own1[t, color, mine]
            for k in range(3):
                total = total + recv2[t, color, k].astype(F32)
            own2[t, color] = total
            lanes = (LEFT, RIGHT)[color]
            for part in range(4):
                piece = own2[t, color, part * PIECE : part * PIECE + PIECE, :]
                own3[t, part, :, lanes] = piece
                send3[t, part, :, lanes] = piece.astype(BF16)
        for k in (2, 1, 3):
            last_copy(t, k).start()

    def finish(t, result):
        for k in (1, 2, 3):
            last_copy(t, k).wait_recv()
        total = own3[t, z]
        for k in range(3):
            total = total + recv3[t, k].astype(F32)
        total = total * scale
        result[pl.ds(0, PIECE, stride=2), :] = total[:, LEFT]
        result[pl.ds(1, PIECE, stride=2), :] = total[:, RIGHT]

    def out_copy(r):
        return pltpu.make_async_copy(stage.at[span(r - 1)], out.at[0, r - 1], out_sem.at[r - 1])

    def last(r, count):
        total = conv(h3, lambda a: wt1[a], r, count, True)
        here = span(r - 1, count)
        stage[here, :] = (gv[span(r, count), :].astype(F32) + total * slope[here, :]).astype(BF16)
        for k in range(count):
            out_copy(r + k).start()

    for pair in loads[:4]:
        for copy in pair:
            copy.wait()
    for copy in weights:
        copy.wait()
    turn(wv2, wt2)
    for r in (1, 2, 3, 4):
        prep(r)
    for pair in loads[4:]:
        for copy in pair:
            copy.wait()
    convs(2, 2, 0)
    prep(5)
    prep(6)
    convs(4, 2, 1)
    elem(2, 0, 0)
    elem(3, 0, 1)
    prep(7)
    prep(8)
    convs(6, 2, 0)
    elem(4, 1, 0)
    elem(5, 1, 1)

    @pl.when(row > 0)
    def _():
        for copy in halos_down:
            copy.wait_recv()

    @pl.when(row == 0)
    def _():
        fv[span(0), :] = jnp.zeros((COLS, CHANS), BF16)
        gv[span(0), :] = jnp.zeros((COLS, CHANS), BF16)

    @pl.when(row < 7)
    def _():
        for copy in halos_up:
            copy.wait_recv()

    @pl.when(row == 7)
    def _():
        fv[span(ROWS + 1), :] = jnp.zeros((COLS, CHANS), BF16)
        gv[span(ROWS + 1), :] = jnp.zeros((COLS, CHANS), BF16)

    for a in range(3):
        grads(1, a, 2, 4, True)
    prep(0)
    prep(ROWS + 1)
    turn(wv1, wt1)
    convs(1, 1, 1)
    elem(6, 0, 0)
    convs(ROWS, 1, 2)
    elem(7, 0, 1)
    for a in range(3):
        grads(1, a, 6, 2, False)
    elem(1, 1, 0)
    elem(ROWS, 2, 0)
    hsend[0] = h3[span(1), CHANS : 2 * CHANS]
    hsend[1] = h3[span(ROWS), CHANS : 2 * CHANS]

    @pl.when(row < 7)
    def _():
        h_down.start()

    @pl.when(row > 0)
    def _():
        h_up.start()

    for a in range(3):
        grads(1, a, 1, 1, False)
        grads(1, a, ROWS, 1, False)
        core_start(1, a)
        grade(1 + a)
    grads(0, 0, 1, ROWS, True)
    core_start(0, 0)
    grade(4)
    grade(5)
    for a in range(3):
        core_add(1, a)
    start1(1)
    grads(0, 1, 1, ROWS, True)
    core_start(0, 1)
    grade(6)
    grade(7)
    grads(0, 2, 1, ROWS, True)
    core_start(0, 2)
    core_add(0, 0)
    core_add(0, 1)
    grade(8)
    last(2, 2)
    core_add(0, 2)
    start1(0)
    start2(1)
    last(4, 2)
    start3(1)
    last(6, 2)

    @pl.when(row > 0)
    def _():
        h_down.wait_recv()

    @pl.when(row == 0)
    def _():
        hrecv[0] = jnp.zeros((COLS, CHANS), BF16)

    @pl.when(row < 7)
    def _():
        h_up.wait_recv()

    @pl.when(row == 7)
    def _():
        hrecv[1] = jnp.zeros((COLS, CHANS), BF16)

    start2(0)
    for end in range(2):
        for lane in (0, 128):
            widen_grad(end * (ROWS + 1), lane, hrecv[end, :, lane : lane + 128].astype(F32))
    last(1, 1)
    finish(1, out_two)
    start3(0)
    last(ROWS, 1)
    finish(0, out_one)

    @pl.when(row < 7)
    def _():
        for copy in halos_down + [h_down]:
            copy.wait_send()

    @pl.when(row > 0)
    def _():
        for copy in halos_up + [h_up]:
            copy.wait_send()

    for r in range(ROWS):
        out_copy(r + 1).wait()
    for t in range(2):
        for g in range(8):
            core_copy(t, g).wait_send()
        for k in (1, 2, 3):
            for color in range(2):
                for step in range(2):
                    wide_copy(t, color, step, k).wait_send()
            last_copy(t, k).wait_send()


def shards(features, cotangent, weight_one, weight_two):
    height = features.shape[1] * lax.axis_size("row")
    scale = 1.0 / math.sqrt(lax.axis_size("img") * height * features.shape[2])
    hbm = pl.BlockSpec(memory_space=pl.ANY)
    vmem = pl.BlockSpec(memory_space=pltpu.VMEM)
    dma = pltpu.SemaphoreType.DMA
    wide_cells = (ROWS + 2) * COLS
    grad, one, two = pl.pallas_call(
        functools.partial(kernel, scale),
        out_shape=(
            jax.ShapeDtypeStruct(features.shape, BF16),
            jax.ShapeDtypeStruct((2 * PIECE, 128), F32),
            jax.ShapeDtypeStruct((2 * PIECE, 128), F32),
        ),
        in_specs=[hbm] * 4,
        out_specs=(hbm, vmem, vmem),
        scratch_shapes=[
            pltpu.VMEM((wide_cells, CHANS), BF16),
            pltpu.VMEM((wide_cells, CHANS), BF16),
            pltpu.VMEM((3, 3, CHANS, CHANS), BF16),
            pltpu.VMEM((3, 3, CHANS, CHANS), BF16),
            pltpu.VMEM((3, WIDE, CHANS), BF16),
            pltpu.VMEM((3, WIDE, CHANS), BF16),
            pltpu.VMEM((wide_cells, WIDE), BF16),
            pltpu.VMEM((wide_cells, WIDE), BF16),
            pltpu.VMEM((wide_cells, WIDE), BF16),
            pltpu.VMEM((CHANS, wide_cells), BF16),
            pltpu.VMEM((CHANS, CELLS), BF16),
            pltpu.VMEM((CELLS, CHANS), F32),
            pltpu.VMEM((3, 2 * COLS, CHANS), F32),
            pltpu.VMEM((3, 2 * COLS, CHANS), F32),
            pltpu.VMEM((2, COLS, CHANS), BF16),
            pltpu.VMEM((2, COLS, CHANS), BF16),
            pltpu.VMEM((CELLS, CHANS), BF16),
            pltpu.VMEM((2, 9 * CHANS, CHANS), F32),
            pltpu.VMEM((2, 8, GROUP, CHANS), F32),
            pltpu.VMEM((2, 2, 4, 2 * GROUP, 128), BF16),
            pltpu.VMEM((2, 2, 3, 2 * GROUP, 128), BF16),
            pltpu.VMEM((2, 2, 4, GROUP // 2, 128), F32),
            pltpu.VMEM((2, 2, 4, GROUP // 2, 128), BF16),
            pltpu.VMEM((2, 2, 3, GROUP // 2, 128), BF16),
            pltpu.VMEM((2, 2, GROUP // 2, 128), F32),
            pltpu.VMEM((2, 4, PIECE, CHANS), BF16),
            pltpu.VMEM((2, 3, PIECE, CHANS), BF16),
            pltpu.VMEM((2, 4, PIECE, CHANS), F32),
            dma((2, ROWS)),
            dma((2,)),
            dma((3, 2)),
            dma((3, 2)),
            dma((ROWS,)),
            dma((2, 8)),
            dma((2, 8)),
            dma((2, 2, 2, 3)),
            dma((2, 2, 2, 3)),
            dma((2, 3)),
            dma((2, 3)),
        ],
        compiler_params=pltpu.CompilerParams(
            collective_id=0, has_side_effects=True, vmem_limit_bytes=64 * 1000 * 1000
        ),
        name="unit_backward",
    )(features, cotangent, weight_one, weight_two)
    return grad, one.reshape(-1), two.reshape(-1)


def solution(mesh):
    placed = (P("img", "row", None, None), P("img", "row", None, None), P(), P())
    return jax.shard_map(
        shards,
        mesh=mesh,
        in_specs=placed,
        out_specs=(P("img", "row", None, None), P(("img", "row")), P(("img", "row"))),
        check_vma=False,
    )
```

```python
import functools
import math

import jax
import jax.numpy as jnp
from jax import lax
from jax.experimental import pallas as pl
from jax.experimental.pallas import tpu as pltpu
from jax.sharding import PartitionSpec as P

MESH = pl.DeviceIdType.MESH
F32 = jnp.float32
BF16 = jnp.bfloat16
COEFF = 0.7978845608028654
CUBIC = 0.044715
ROWS = 8
COLS = 384
CHANS = 256
WIDE = 3 * CHANS
CELLS = ROWS * COLS
GROUP = 144
PIECE = 18


def gelu_terms(v):
    poly = COEFF + (COEFF * CUBIC) * (v * v)
    half = 0.5 + 0.5 * jnp.tanh(v * poly)
    return v * half, half, poly


def slope_of(acted, half, poly):
    return half + acted * (1.0 - half) * (6.0 * poly - 4.0 * COEFF)


def span(row, count=1):
    return slice(row * COLS, (row + count) * COLS)


def rows_of(refs, rows, columns):
    return jnp.concatenate([refs[r][:, columns] for r in rows], axis=0)


def lanes_of(refs, rows):
    return jnp.concatenate([refs[r][...] for r in rows], axis=1)


def weave(*streams):
    longest = max(len(stream) for stream in streams)
    done = [0] * len(streams)
    for step in range(longest):
        for k, stream in enumerate(streams):
            end = (step + 1) * len(stream) // longest
            for task in stream[done[k] : end]:
                task()
            done[k] = end


def kernel(
    scale,
    feat,
    cot,
    w_one,
    w_two,
    out,
    out_one,
    out_two,
    fv,
    gv,
    wv1,
    wv2,
    wt1,
    wt2,
    a3,
    g3,
    h3,
    at,
    gt,
    slope,
    hid,
    bh,
    hsend,
    hrecv,
    stage,
    acc,
    crecv,
    send1,
    recv1,
    own1,
    send2,
    recv2,
    own2,
    send3,
    recv3,
    own3,
    load_sem,
    w_sem,
    halo_send,
    halo_recv,
    out_sem,
    core_send,
    core_recv,
    wide_send,
    wide_recv,
    last_send,
    last_recv,
):
    img, row = lax.axis_index("img"), lax.axis_index("row")
    core, y_lo, x = img % 2, (img // 2) % 2, img // 4
    z, y_hi = row % 4, row // 4
    y = y_hi * 2 + y_lo

    def x_peer(k):
        there = (x + k) % 4
        return there, ((there * 2 + y_lo) * 2 + core, row)

    def y_peer(k):
        there = (y + k) % 4
        return there, ((x * 2 + there % 2) * 2 + core, (there // 2) * 4 + z)

    def z_peer(k):
        there = (z + k) % 4
        return there, (img, y_hi * 4 + there)

    partner = ((x * 2 + y_lo) * 2 + (1 - core), row)
    below, above = (img, (row + 1) % 8), (img, (row + 7) % 8)

    loads = [
        (
            pltpu.make_async_copy(feat.at[0, r], fv[r + 1], load_sem.at[0, r]),
            pltpu.make_async_copy(cot.at[0, r], gv[r + 1], load_sem.at[1, r]),
        )
        for r in range(ROWS)
    ]
    weights = [
        pltpu.make_async_copy(w_one, wv1, w_sem.at[0]),
        pltpu.make_async_copy(w_two, wv2, w_sem.at[1]),
    ]
    for pair in loads[:4]:
        for copy in pair:
            copy.start()
    for copy in weights:
        copy.start()
    for pair in loads[4:]:
        for copy in pair:
            copy.start()

    barrier = pltpu.get_barrier_semaphore()
    peers = [partner, below, above]
    for peer in (x_peer, y_peer, z_peer):
        for k in (1, 2, 3):
            peers.append(peer(k)[1])
    for peer in peers:
        pl.semaphore_signal(barrier, inc=1, device_id=peer, device_id_type=MESH)
    pl.semaphore_wait(barrier, len(peers))

    def halo(which, down, src, dst):
        return pltpu.make_async_remote_copy(
            src_ref=src,
            dst_ref=dst,
            send_sem=halo_send.at[which, down],
            recv_sem=halo_recv.at[which, down],
            device_id=below if down else above,
            device_id_type=MESH,
        )

    halos_down = [
        halo(0, 1, feat.at[0, ROWS - 1], fv[0]),
        halo(1, 1, cot.at[0, ROWS - 1], gv[0]),
    ]
    halos_up = [
        halo(0, 0, feat.at[0, 0], fv[ROWS + 1]),
        halo(1, 0, cot.at[0, 0], gv[ROWS + 1]),
    ]
    h_down = halo(2, 1, hsend.at[1], hrecv.at[0])
    h_up = halo(2, 0, hsend.at[0], hrecv.at[1])

    @pl.when(row < 7)
    def _():
        for copy in halos_down:
            copy.start()

    @pl.when(row > 0)
    def _():
        for copy in halos_up:
            copy.start()

    def turn(source, target):
        def block(a, b):
            target[a, b * CHANS : (b + 1) * CHANS, :] = source[a, b].T

        return [functools.partial(block, a, b) for a in range(3) for b in range(3)]

    def window(ref, lane, c):
        blank = jnp.zeros((8, 128), F32)
        low, high = 128 * c - 8, 128 * c + 136
        inside = ref[max(low, 0) : min(high, COLS), lane : lane + 128].astype(F32)
        if c == 0:
            inside = jnp.concatenate([blank, inside], axis=0)
        if c == 2:
            inside = jnp.concatenate([inside, blank], axis=0)
        return pltpu.roll(inside, 1, 0)[8:136], pltpu.roll(inside, 143, 0)[8:136]

    def block(lane, c):
        return slice(128 * c, 128 * c + 128), slice(lane, lane + 128)

    def wide_block(lane, c, tap):
        return slice(128 * c, 128 * c + 128), slice(tap * CHANS + lane, tap * CHANS + lane + 128)

    def acted_one(r, lane, c):
        acted, _, _ = gelu_terms(fv[r][block(lane, c)].astype(F32))
        mid = acted.astype(BF16)
        hid[r][block(lane, c)] = acted
        a3[r][wide_block(lane, c, 1)] = mid
        at[r][lane : lane + 128, 128 * c : 128 * c + 128] = mid.T

    def acted_two(r, lane, c):
        left, right = window(hid[r], lane, c)
        a3[r][wide_block(lane, c, 0)] = left.astype(BF16)
        a3[r][wide_block(lane, c, 2)] = right.astype(BF16)

    def cot_one(r, lane, c):
        left, right = window(gv[r], lane, c)
        g3[r][wide_block(lane, c, 0)] = right.astype(BF16)
        g3[r][wide_block(lane, c, 1)] = gv[r][block(lane, c)]
        g3[r][wide_block(lane, c, 2)] = left.astype(BF16)

    def grade_one(r, lane, c):
        slope[r][block(lane, c)] = slope_of(*gelu_terms(fv[r][block(lane, c)].astype(F32)))

    def elem_one(r, lane, c):
        terms = gelu_terms(hid[r][block(lane, c)])
        gt[r][lane : lane + 128, 128 * c : 128 * c + 128] = terms[0].astype(BF16).T
        grad = bh[r][block(lane, c)] * slope_of(*terms)
        bh[r][block(lane, c)] = grad
        h3[r][wide_block(lane, c, 1)] = grad.astype(BF16)

    def elem_two(r, lane, c):
        left, right = window(bh[r], lane, c)
        h3[r][wide_block(lane, c, 0)] = right.astype(BF16)
        h3[r][wide_block(lane, c, 2)] = left.astype(BF16)

    def halo_one(r, lane, c):
        left, right = window(hrecv.at[r // ROWS], lane, c)
        h3[r][wide_block(lane, c, 0)] = right.astype(BF16)
        h3[r][wide_block(lane, c, 1)] = hrecv[r // ROWS, 128 * c : 128 * c + 128, lane : lane + 128]
        h3[r][wide_block(lane, c, 2)] = left.astype(BF16)

    def single(task, *rows):
        return [functools.partial(task, r, lane, c) for r in rows for lane in (0, 128) for c in range(3)]

    def double(one, two, *rows):
        order = ((one, 0), (one, 1), (two, 0), (one, 2), (two, 1), (two, 2))
        return [functools.partial(f, r, lane, c) for r in rows for lane in (0, 128) for f, c in order]

    def acted(*rows):
        return double(acted_one, acted_two, *rows)

    def elem(*rows):
        return double(elem_one, elem_two, *rows)

    def cots(*rows):
        return single(cot_one, *rows)

    def grade(*rows):
        return single(grade_one, *rows)

    def both(*streams):
        def step(tasks):
            for task in tasks:
                task()

        return [functools.partial(step, tasks) for tasks in zip(*streams, strict=True)]

    def conv(source, weight, rows, flip, keep):
        box = [None]

        def step(a, b):
            near = [r - a + 1 if flip else r + a - 1 for r in rows]
            columns = slice(b * CHANS, (b + 1) * CHANS)
            part = jnp.dot(rows_of(source, near, columns), weight(a, b), preferred_element_type=F32)
            box[0] = part if box[0] is None else box[0] + part
            if (a, b) == (2, 2):
                keep(box[0])

        return [functools.partial(step, a, b) for a in range(3) for b in range(3)]

    def keep_in(refs, rows):
        def keep(total):
            for k, r in enumerate(rows):
                refs[r][...] = total[span(k), :]

        return keep

    def forward(*rows):
        return conv(a3, lambda a, b: wv1[a, b], rows, False, keep_in(hid, rows))

    def backward(*rows):
        return conv(
            g3, lambda a, b: wt2[a, b * CHANS : (b + 1) * CHANS, :], rows, True, keep_in(bh, rows)
        )

    def grads(t, fresh, terms, taps=(0, 1, 2)):
        tall = len(taps) * CHANS

        def build(b, low, high):
            box = [None]

            def step(pair, part, final):
                lhs = jnp.concatenate([lanes_of(*pair[k]) for k in range(len(taps))], axis=0)[low:high]
                rhs = rows_of(pair[-1][0], pair[-1][1], slice(b * CHANS, (b + 1) * CHANS))
                deep = slice(part * CHANS, (part + 1) * CHANS)
                product = jnp.dot(lhs[:, deep], rhs[deep, :], preferred_element_type=F32)
                box[0] = product if box[0] is None else box[0] + product
                if final:
                    for k, a in enumerate(taps):
                        start, end = max(low, k * CHANS), min(high, (k + 1) * CHANS)
                        if start < end:
                            base = (a * 3 + b) * CHANS - k * CHANS
                            here = slice(base + start, base + end)
                            piece = box[0][start - low : end - low, :]
                            acc[t, here, :] = piece if fresh else acc[t, here, :] + piece

            return [
                functools.partial(step, pair, part, pair is terms[-1] and part == 2)
                for pair in terms
                for part in range(3)
            ]

        half = tall // 2
        return both(build(0, 0, tall), build(1, 0, tall)) + both(build(2, 0, half), build(2, half, tall))

    def one_grads(fresh, *pairs):
        terms = [[(at, (p + a - 1, q + a - 1)) for a in range(3)] + [(h3, (p, q))] for p, q in pairs]
        return grads(0, fresh, terms)

    def two_grads(*pairs):
        terms = [[(gt, (p + a - 1, q + a - 1)) for a in range(3)] + [(g3, (p, q))] for p, q in pairs]
        return grads(1, True, terms)

    def two_edge(a, left, right):
        return grads(1, False, [[(gt, left), (g3, right)]], (a,))

    def core_copy(t, g):
        return pltpu.make_async_remote_copy(
            src_ref=acc.at[t, pl.ds(pl.multiple_of((2 * g + 1 - core) * GROUP, GROUP), GROUP)],
            dst_ref=crecv.at[t, g],
            send_sem=core_send.at[t, g],
            recv_sem=core_recv.at[t, g],
            device_id=partner,
            device_id_type=MESH,
        )

    def wide_copy(t, color, step, k):
        send, recv = ((send1, recv1), (send2, recv2))[step]
        there, device = (x_peer if color == step else y_peer)(k)
        return pltpu.make_async_remote_copy(
            src_ref=send.at[t, color, there],
            dst_ref=recv.at[t, color, k - 1],
            send_sem=wide_send.at[t, color, step, k - 1],
            recv_sem=wide_recv.at[t, color, step, k - 1],
            device_id=device,
            device_id_type=MESH,
        )

    def last_copy(t, k):
        there, device = z_peer(k)
        return pltpu.make_async_remote_copy(
            src_ref=send3.at[t, there],
            dst_ref=recv3.at[t, k - 1],
            send_sem=last_send.at[t, k - 1],
            recv_sem=last_recv.at[t, k - 1],
            device_id=device,
            device_id_type=MESH,
        )

    HALF = GROUP // 2
    LEFT, RIGHT = slice(0, 128), slice(128, 256)

    def core_start(t):
        for g in range(8):
            core_copy(t, g).start()

    def core_add(t, g):
        core_copy(t, g).wait_recv()
        here = pl.ds(pl.multiple_of((2 * g + core) * GROUP, GROUP), GROUP)
        total = acc[t, here, :] + crecv[t, g]
        crecv[t, g] = total
        place, low = g // 2, g % 2
        send1[t, 0, place, low * GROUP : (low + 1) * GROUP, :] = total[:, LEFT].astype(BF16)
        for high in range(2):
            send1[t, 1, high * 2 + low, place * HALF : (place + 1) * HALF, :] = total[
                high * HALF : (high + 1) * HALF, RIGHT
            ].astype(BF16)

    def start1(t):
        for k in (2, 1, 3):
            for color in range(2):
                wide_copy(t, color, 0, k).start()

    def start2(t):
        for color in range(2):
            for k in (1, 2, 3):
                wide_copy(t, color, 0, k).wait_recv()
        for low in range(2):
            for high in range(2):
                rows = slice(low * GROUP + high * HALF, low * GROUP + (high + 1) * HALF)
                total = crecv[t, 2 * x + low, high * HALF : (high + 1) * HALF, LEFT]
                for k in range(3):
                    total = total + recv1[t, 0, k, rows, :].astype(F32)
                own1[t, 0, high * 2 + low] = total
                send2[t, 0, high * 2 + low] = total.astype(BF16)
        for place in range(4):
            rows = slice(place * HALF, (place + 1) * HALF)
            total = crecv[t, 2 * place + y_lo, pl.ds(pl.multiple_of(y_hi * HALF, HALF), HALF), RIGHT]
            for k in range(3):
                total = total + recv1[t, 1, k, rows, :].astype(F32)
            own1[t, 1, place] = total
            send2[t, 1, place] = total.astype(BF16)
        for k in (2, 1, 3):
            for color in range(2):
                wide_copy(t, color, 1, k).start()

    def start3(t):
        for color, mine in ((0, y), (1, x)):
            for k in (1, 2, 3):
                wide_copy(t, color, 1, k).wait_recv()
            total = own1[t, color, mine]
            for k in range(3):
                total = total + recv2[t, color, k].astype(F32)
            own2[t, color] = total
            lanes = (LEFT, RIGHT)[color]
            for part in range(4):
                piece = own2[t, color, part * PIECE : part * PIECE + PIECE, :]
                own3[t, part, :, lanes] = piece
                send3[t, part, :, lanes] = piece.astype(BF16)
        for k in (2, 1, 3):
            last_copy(t, k).start()

    def finish(t, result):
        for k in (1, 2, 3):
            last_copy(t, k).wait_recv()
        total = own3[t, z]
        for k in range(3):
            total = total + recv3[t, k].astype(F32)
        total = total * scale
        result[pl.ds(0, PIECE, stride=2), :] = total[:, LEFT]
        result[pl.ds(1, PIECE, stride=2), :] = total[:, RIGHT]

    def out_copy(r):
        return pltpu.make_async_copy(stage[r], out.at[0, r - 1], out_sem.at[r - 1])

    def last(*rows):
        def keep(total):
            for k, r in enumerate(rows):
                stage[r][...] = (gv[r][...].astype(F32) + total[span(k), :] * slope[r][...]).astype(BF16)
                out_copy(r).start()

        return conv(h3, lambda a, b: wt1[a, b * CHANS : (b + 1) * CHANS, :], rows, True, keep)

    for pair in loads[:4]:
        for copy in pair:
            copy.wait()
    weights[1].wait()
    weave(turn(wv2, wt2), cots(1, 2, 3, 4))
    weave(both(backward(2), backward(3)), acted(1, 2, 3, 4))
    weights[0].wait()
    for pair in loads[4:]:
        for copy in pair:
            copy.wait()
    weave(both(forward(2), forward(3)), cots(5, 6, 7, 8) + acted(5, 6))
    weave(both(forward(4, 5), backward(4, 5)), acted(7, 8) + elem(2))
    weave(both(forward(6, 7), backward(6, 7)), elem(3, 4, 5), turn(wv1, wt1))

    @pl.when(row > 0)
    def _():
        for copy in halos_down:
            copy.wait_recv()

    @pl.when(row == 0)
    def _():
        fv[0][...] = jnp.zeros((COLS, CHANS), BF16)
        gv[0][...] = jnp.zeros((COLS, CHANS), BF16)

    @pl.when(row < 7)
    def _():
        for copy in halos_up:
            copy.wait_recv()

    @pl.when(row == 7)
    def _():
        fv[ROWS + 1][...] = jnp.zeros((COLS, CHANS), BF16)
        gv[ROWS + 1][...] = jnp.zeros((COLS, CHANS), BF16)

    weave(one_grads(True, (2, 3), (4, 5)), cots(0, ROWS + 1) + acted(0, ROWS + 1) + elem(6, 7))
    weave(both(forward(1, ROWS), backward(1, ROWS)), grade(1, 2, 3, 4, 5))
    weave(one_grads(False, (6, 7)), elem(1, ROWS))
    hsend[0] = h3[1][:, CHANS : 2 * CHANS]
    hsend[1] = h3[ROWS][:, CHANS : 2 * CHANS]

    @pl.when(row < 7)
    def _():
        h_down.start()

    @pl.when(row > 0)
    def _():
        h_up.start()

    weave(one_grads(False, (1, ROWS)), grade(6, 7, 8))
    core_start(0)
    inner = two_grads((2, 3), (4, 5), (6, 7))
    weave(inner[:9])
    weave(inner[9:], [functools.partial(core_add, 0, g) for g in range(8)])
    start1(0)
    weave(
        two_edge(1, (1, ROWS), (1, ROWS))
        + two_edge(2, (2, 1), (1, 0))
        + two_edge(0, (ROWS - 1, ROWS), (ROWS, ROWS + 1))
    )
    core_start(1)
    start2(0)
    inner = both(last(2, 3), last(4, 5))
    weave(inner[:5])
    weave(inner[5:], [functools.partial(core_add, 1, g) for g in range(8)])
    start1(1)
    start3(0)

    @pl.when(row > 0)
    def _():
        h_down.wait_recv()

    @pl.when(row == 0)
    def _():
        hrecv[0] = jnp.zeros((COLS, CHANS), BF16)

    @pl.when(row < 7)
    def _():
        h_up.wait_recv()

    @pl.when(row == 7)
    def _():
        hrecv[1] = jnp.zeros((COLS, CHANS), BF16)

    inner = both(last(6, 7), last(1, ROWS))
    weave(single(halo_one, 0, ROWS + 1))
    weave(inner[:3])
    start2(1)
    weave(inner[3:7])
    finish(0, out_one)
    start3(1)
    weave(inner[7:])
    finish(1, out_two)

    @pl.when(row < 7)
    def _():
        for copy in halos_down + [h_down]:
            copy.wait_send()

    @pl.when(row > 0)
    def _():
        for copy in halos_up + [h_up]:
            copy.wait_send()

    for r in range(ROWS):
        out_copy(r + 1).wait()
    for t in range(2):
        for g in range(8):
            core_copy(t, g).wait_send()
        for k in (1, 2, 3):
            for color in range(2):
                for step in range(2):
                    wide_copy(t, color, step, k).wait_send()
            last_copy(t, k).wait_send()


def shards(features, cotangent, weight_one, weight_two):
    height = features.shape[1] * lax.axis_size("row")
    scale = 1.0 / math.sqrt(lax.axis_size("img") * height * features.shape[2])
    hbm = pl.BlockSpec(memory_space=pl.ANY)
    vmem = pl.BlockSpec(memory_space=pltpu.VMEM)
    dma = pltpu.SemaphoreType.DMA
    wide = ROWS + 2
    grad, one, two = pl.pallas_call(
        functools.partial(kernel, scale),
        out_shape=(
            jax.ShapeDtypeStruct(features.shape, BF16),
            jax.ShapeDtypeStruct((2 * PIECE, 128), F32),
            jax.ShapeDtypeStruct((2 * PIECE, 128), F32),
        ),
        in_specs=[hbm] * 4,
        out_specs=(hbm, vmem, vmem),
        scratch_shapes=[
            [pltpu.VMEM((COLS, CHANS), BF16)] * wide,
            [pltpu.VMEM((COLS, CHANS), BF16)] * wide,
            pltpu.VMEM((3, 3, CHANS, CHANS), BF16),
            pltpu.VMEM((3, 3, CHANS, CHANS), BF16),
            pltpu.VMEM((3, WIDE, CHANS), BF16),
            pltpu.VMEM((3, WIDE, CHANS), BF16),
            [pltpu.VMEM((COLS, WIDE), BF16)] * wide,
            [pltpu.VMEM((COLS, WIDE), BF16)] * wide,
            [pltpu.VMEM((COLS, WIDE), BF16)] * wide,
            [pltpu.VMEM((CHANS, COLS), BF16)] * wide,
            [pltpu.VMEM((CHANS, COLS), BF16)] * wide,
            [pltpu.VMEM((COLS, CHANS), F32)] * wide,
            [pltpu.VMEM((COLS, CHANS), F32)] * wide,
            [pltpu.VMEM((COLS, CHANS), F32)] * wide,
            pltpu.VMEM((2, COLS, CHANS), BF16),
            pltpu.VMEM((2, COLS, CHANS), BF16),
            [pltpu.VMEM((COLS, CHANS), BF16)] * wide,
            pltpu.VMEM((2, 9 * CHANS, CHANS), F32),
            pltpu.VMEM((2, 8, GROUP, CHANS), F32),
            pltpu.VMEM((2, 2, 4, 2 * GROUP, 128), BF16),
            pltpu.VMEM((2, 2, 3, 2 * GROUP, 128), BF16),
            pltpu.VMEM((2, 2, 4, GROUP // 2, 128), F32),
            pltpu.VMEM((2, 2, 4, GROUP // 2, 128), BF16),
            pltpu.VMEM((2, 2, 3, GROUP // 2, 128), BF16),
            pltpu.VMEM((2, 2, GROUP // 2, 128), F32),
            pltpu.VMEM((2, 4, PIECE, CHANS), BF16),
            pltpu.VMEM((2, 3, PIECE, CHANS), BF16),
            pltpu.VMEM((2, 4, PIECE, CHANS), F32),
            dma((2, ROWS)),
            dma((2,)),
            dma((3, 2)),
            dma((3, 2)),
            dma((ROWS,)),
            dma((2, 8)),
            dma((2, 8)),
            dma((2, 2, 2, 3)),
            dma((2, 2, 2, 3)),
            dma((2, 3)),
            dma((2, 3)),
        ],
        compiler_params=pltpu.CompilerParams(
            collective_id=0, has_side_effects=True, vmem_limit_bytes=64 * 1000 * 1000
        ),
        name="unit_backward",
    )(features, cotangent, weight_one, weight_two)
    return grad, one.reshape(-1), two.reshape(-1)


def solution(mesh):
    placed = (P("img", "row", None, None), P("img", "row", None, None), P(), P())
    return jax.shard_map(
        shards,
        mesh=mesh,
        in_specs=placed,
        out_specs=(P("img", "row", None, None), P(("img", "row")), P(("img", "row"))),
        check_vma=False,
    )
```

```python
import functools
import math

import jax
import jax.numpy as jnp
from jax import lax
from jax.experimental import pallas as pl
from jax.experimental.pallas import tpu as pltpu
from jax.sharding import PartitionSpec as P

MESH = pl.DeviceIdType.MESH
F32 = jnp.float32
BF16 = jnp.bfloat16
COEFF = 0.7978845608028654
CUBIC = 0.044715
ROWS = 8
COLS = 384
CHANS = 256
WIDE = 3 * CHANS
CELLS = ROWS * COLS
GROUP = 144
PIECE = 18


def gelu_terms(v):
    poly = COEFF + (COEFF * CUBIC) * (v * v)
    half = 0.5 + 0.5 * jnp.tanh(v * poly)
    return v * half, half, poly


def slope_of(acted, half, poly):
    return half + acted * (1.0 - half) * (6.0 * poly - 4.0 * COEFF)


def span(row, count=1):
    return slice(row * COLS, (row + count) * COLS)


def rows_of(refs, rows, columns):
    return jnp.concatenate([refs[r][:, columns] for r in rows], axis=0)


def lanes_of(refs, rows):
    return jnp.concatenate([refs[r][...] for r in rows], axis=1)


def weave(*streams):
    longest = max(len(stream) for stream in streams)
    done = [0] * len(streams)
    for step in range(longest):
        for k, stream in enumerate(streams):
            end = (step + 1) * len(stream) // longest
            for task in stream[done[k] : end]:
                task()
            done[k] = end


def kernel(
    scale,
    feat,
    cot,
    w_one,
    w_two,
    out,
    out_one,
    out_two,
    fv,
    gv,
    wv1,
    wv2,
    wt1,
    wt2,
    a3,
    g3,
    h3,
    at,
    gt,
    slope,
    hid,
    bh,
    hsend,
    hrecv,
    stage,
    acc,
    crecv,
    send1,
    recv1,
    own1,
    send2,
    recv2,
    own2,
    send3,
    recv3,
    own3,
    load_sem,
    w_sem,
    halo_send,
    halo_recv,
    out_sem,
    core_send,
    core_recv,
    wide_send,
    wide_recv,
    last_send,
    last_recv,
):
    img, row = lax.axis_index("img"), lax.axis_index("row")
    core, y_lo, x = img % 2, (img // 2) % 2, img // 4
    z, y_hi = row % 4, row // 4
    y = y_hi * 2 + y_lo

    def x_peer(k):
        there = (x + k) % 4
        return there, ((there * 2 + y_lo) * 2 + core, row)

    def y_peer(k):
        there = (y + k) % 4
        return there, ((x * 2 + there % 2) * 2 + core, (there // 2) * 4 + z)

    def z_peer(k):
        there = (z + k) % 4
        return there, (img, y_hi * 4 + there)

    partner = ((x * 2 + y_lo) * 2 + (1 - core), row)
    below, above = (img, (row + 1) % 8), (img, (row + 7) % 8)

    loads = [
        (
            pltpu.make_async_copy(feat.at[0, r], fv[r + 1], load_sem.at[0, r]),
            pltpu.make_async_copy(cot.at[0, r], gv[r + 1], load_sem.at[1, r]),
        )
        for r in range(ROWS)
    ]
    weights = [
        pltpu.make_async_copy(w_one, wv1, w_sem.at[0]),
        pltpu.make_async_copy(w_two, wv2, w_sem.at[1]),
    ]
    for pair in loads[:4]:
        for copy in pair:
            copy.start()
    for copy in weights:
        copy.start()
    for pair in loads[4:]:
        for copy in pair:
            copy.start()

    barrier = pltpu.get_barrier_semaphore()
    peers = [partner, below, above]
    for peer in (x_peer, y_peer, z_peer):
        for k in (1, 2, 3):
            peers.append(peer(k)[1])
    for peer in peers:
        pl.semaphore_signal(barrier, inc=1, device_id=peer, device_id_type=MESH)

    def halo(which, down, src, dst):
        return pltpu.make_async_remote_copy(
            src_ref=src,
            dst_ref=dst,
            send_sem=halo_send.at[which, down],
            recv_sem=halo_recv.at[which, down],
            device_id=below if down else above,
            device_id_type=MESH,
        )

    halos_down = [
        halo(0, 1, feat.at[0, ROWS - 1], fv[0]),
        halo(1, 1, cot.at[0, ROWS - 1], gv[0]),
    ]
    halos_up = [
        halo(0, 0, feat.at[0, 0], fv[ROWS + 1]),
        halo(1, 0, cot.at[0, 0], gv[ROWS + 1]),
    ]
    h_down = halo(2, 1, hsend.at[1], hrecv.at[0])
    h_up = halo(2, 0, hsend.at[0], hrecv.at[1])

    def turn(source, target):
        def block(a, b):
            target[a, b * CHANS : (b + 1) * CHANS, :] = source[a, b].T

        return [functools.partial(block, a, b) for a in range(3) for b in range(3)]

    def window(ref, lane, c):
        blank = jnp.zeros((8, 128), F32)
        low, high = 128 * c - 8, 128 * c + 136
        inside = ref[max(low, 0) : min(high, COLS), lane : lane + 128].astype(F32)
        if c == 0:
            inside = jnp.concatenate([blank, inside], axis=0)
        if c == 2:
            inside = jnp.concatenate([inside, blank], axis=0)
        return pltpu.roll(inside, 1, 0)[8:136], pltpu.roll(inside, 143, 0)[8:136]

    def block(lane, c):
        return slice(128 * c, 128 * c + 128), slice(lane, lane + 128)

    def wide_block(lane, c, tap):
        return slice(128 * c, 128 * c + 128), slice(tap * CHANS + lane, tap * CHANS + lane + 128)

    def acted_one(r, lane, c):
        acted, _, _ = gelu_terms(fv[r][block(lane, c)].astype(F32))
        mid = acted.astype(BF16)
        hid[r][block(lane, c)] = acted
        a3[r][wide_block(lane, c, 1)] = mid
        at[r][lane : lane + 128, 128 * c : 128 * c + 128] = mid.T

    def acted_two(r, lane, c):
        left, right = window(hid[r], lane, c)
        a3[r][wide_block(lane, c, 0)] = left.astype(BF16)
        a3[r][wide_block(lane, c, 2)] = right.astype(BF16)

    def cot_one(r, lane, c):
        left, right = window(gv[r], lane, c)
        g3[r][wide_block(lane, c, 0)] = right.astype(BF16)
        g3[r][wide_block(lane, c, 1)] = gv[r][block(lane, c)]
        g3[r][wide_block(lane, c, 2)] = left.astype(BF16)

    def grade_one(r, lane, c):
        slope[r][block(lane, c)] = slope_of(*gelu_terms(fv[r][block(lane, c)].astype(F32)))

    def elem_one(r, lane, c):
        terms = gelu_terms(hid[r][block(lane, c)])
        gt[r][lane : lane + 128, 128 * c : 128 * c + 128] = terms[0].astype(BF16).T
        grad = bh[r][block(lane, c)] * slope_of(*terms)
        bh[r][block(lane, c)] = grad
        h3[r][wide_block(lane, c, 1)] = grad.astype(BF16)

    def elem_two(r, lane, c):
        left, right = window(bh[r], lane, c)
        h3[r][wide_block(lane, c, 0)] = right.astype(BF16)
        h3[r][wide_block(lane, c, 2)] = left.astype(BF16)

    def halo_one(r, lane, c):
        left, right = window(hrecv.at[r // ROWS], lane, c)
        h3[r][wide_block(lane, c, 0)] = right.astype(BF16)
        h3[r][wide_block(lane, c, 1)] = hrecv[r // ROWS, 128 * c : 128 * c + 128, lane : lane + 128]
        h3[r][wide_block(lane, c, 2)] = left.astype(BF16)

    def single(task, *rows):
        return [functools.partial(task, r, lane, c) for r in rows for lane in (0, 128) for c in range(3)]

    def double(one, two, *rows):
        order = ((one, 0), (one, 1), (two, 0), (one, 2), (two, 1), (two, 2))
        return [functools.partial(f, r, lane, c) for r in rows for lane in (0, 128) for f, c in order]

    def acted(*rows):
        return double(acted_one, acted_two, *rows)

    def elem(*rows):
        return double(elem_one, elem_two, *rows)

    def cots(*rows):
        return single(cot_one, *rows)

    def grade(*rows):
        return single(grade_one, *rows)

    def both(*streams):
        def step(tasks):
            for task in tasks:
                task()

        return [functools.partial(step, tasks) for tasks in zip(*streams, strict=True)]

    def conv(source, weight, rows, flip, keep):
        box = [None]

        def step(a, b):
            near = [r - a + 1 if flip else r + a - 1 for r in rows]
            columns = slice(b * CHANS, (b + 1) * CHANS)
            part = jnp.dot(rows_of(source, near, columns), weight(a, b), preferred_element_type=F32)
            box[0] = part if box[0] is None else box[0] + part
            if (a, b) == (2, 2):
                keep(box[0])

        return [functools.partial(step, a, b) for a in range(3) for b in range(3)]

    def keep_in(refs, rows):
        def keep(total):
            for k, r in enumerate(rows):
                refs[r][...] = total[span(k), :]

        return keep

    def forward(*rows):
        return conv(a3, lambda a, b: wv1[a, b], rows, False, keep_in(hid, rows))

    def backward(*rows):
        return conv(
            g3, lambda a, b: wt2[a, b * CHANS : (b + 1) * CHANS, :], rows, True, keep_in(bh, rows)
        )

    def grads(t, fresh, terms, taps=(0, 1, 2)):
        tall = len(taps) * CHANS

        def build(b, low, high):
            box = [None]

            def step(pair, part, final):
                lhs = jnp.concatenate([lanes_of(*pair[k]) for k in range(len(taps))], axis=0)[low:high]
                rhs = rows_of(pair[-1][0], pair[-1][1], slice(b * CHANS, (b + 1) * CHANS))
                deep = slice(part * CHANS, (part + 1) * CHANS)
                product = jnp.dot(lhs[:, deep], rhs[deep, :], preferred_element_type=F32)
                box[0] = product if box[0] is None else box[0] + product
                if final:
                    for k, a in enumerate(taps):
                        start, end = max(low, k * CHANS), min(high, (k + 1) * CHANS)
                        if start < end:
                            base = (a * 3 + b) * CHANS - k * CHANS
                            here = slice(base + start, base + end)
                            piece = box[0][start - low : end - low, :]
                            acc[t, here, :] = piece if fresh else acc[t, here, :] + piece

            return [
                functools.partial(step, pair, part, pair is terms[-1] and part == 2)
                for pair in terms
                for part in range(3)
            ]

        half = tall // 2
        return both(build(0, 0, tall), build(1, 0, tall)) + both(build(2, 0, half), build(2, half, tall))

    def one_grads(fresh, *pairs):
        terms = [[(at, (p + a - 1, q + a - 1)) for a in range(3)] + [(h3, (p, q))] for p, q in pairs]
        return grads(0, fresh, terms)

    def two_grads(fresh, *pairs):
        terms = [[(gt, (p + a - 1, q + a - 1)) for a in range(3)] + [(g3, (p, q))] for p, q in pairs]
        return grads(1, fresh, terms)

    def two_edge(a, left, right):
        return grads(1, False, [[(gt, left), (g3, right)]], (a,))

    def core_copy(t, g):
        return pltpu.make_async_remote_copy(
            src_ref=acc.at[t, pl.ds(pl.multiple_of((2 * g + 1 - core) * GROUP, GROUP), GROUP)],
            dst_ref=crecv.at[t, g],
            send_sem=core_send.at[t, g],
            recv_sem=core_recv.at[t, g],
            device_id=partner,
            device_id_type=MESH,
        )

    def wide_copy(t, color, step, k):
        send, recv = ((send1, recv1), (send2, recv2))[step]
        there, device = (x_peer if color == step else y_peer)(k)
        return pltpu.make_async_remote_copy(
            src_ref=send.at[t, color, there],
            dst_ref=recv.at[t, color, k - 1],
            send_sem=wide_send.at[t, color, step, k - 1],
            recv_sem=wide_recv.at[t, color, step, k - 1],
            device_id=device,
            device_id_type=MESH,
        )

    def last_copy(t, k):
        there, device = z_peer(k)
        return pltpu.make_async_remote_copy(
            src_ref=send3.at[t, there],
            dst_ref=recv3.at[t, k - 1],
            send_sem=last_send.at[t, k - 1],
            recv_sem=last_recv.at[t, k - 1],
            device_id=device,
            device_id_type=MESH,
        )

    HALF = GROUP // 2
    LEFT, RIGHT = slice(0, 128), slice(128, 256)

    def core_start(t, groups):
        for g in groups:
            core_copy(t, g).start()

    def core_add(t, g):
        core_copy(t, g).wait_recv()
        here = pl.ds(pl.multiple_of((2 * g + core) * GROUP, GROUP), GROUP)
        total = acc[t, here, :] + crecv[t, g]
        crecv[t, g] = total
        place, low = g // 2, g % 2
        send1[t, 0, place, low * GROUP : (low + 1) * GROUP, :] = total[:, LEFT].astype(BF16)
        for high in range(2):
            send1[t, 1, high * 2 + low, place * HALF : (place + 1) * HALF, :] = total[
                high * HALF : (high + 1) * HALF, RIGHT
            ].astype(BF16)

    def start1(t):
        for k in (2, 1, 3):
            for color in range(2):
                wide_copy(t, color, 0, k).start()

    def start2(t):
        for color in range(2):
            for k in (1, 2, 3):
                wide_copy(t, color, 0, k).wait_recv()
        for low in range(2):
            for high in range(2):
                rows = slice(low * GROUP + high * HALF, low * GROUP + (high + 1) * HALF)
                total = crecv[t, 2 * x + low, high * HALF : (high + 1) * HALF, LEFT]
                for k in range(3):
                    total = total + recv1[t, 0, k, rows, :].astype(F32)
                own1[t, 0, high * 2 + low] = total
                send2[t, 0, high * 2 + low] = total.astype(BF16)
        for place in range(4):
            rows = slice(place * HALF, (place + 1) * HALF)
            total = crecv[t, 2 * place + y_lo, pl.ds(pl.multiple_of(y_hi * HALF, HALF), HALF), RIGHT]
            for k in range(3):
                total = total + recv1[t, 1, k, rows, :].astype(F32)
            own1[t, 1, place] = total
            send2[t, 1, place] = total.astype(BF16)
        for k in (2, 1, 3):
            for color in range(2):
                wide_copy(t, color, 1, k).start()

    def start3(t):
        for color, mine in ((0, y), (1, x)):
            for k in (1, 2, 3):
                wide_copy(t, color, 1, k).wait_recv()
            total = own1[t, color, mine]
            for k in range(3):
                total = total + recv2[t, color, k].astype(F32)
            own2[t, color] = total
            lanes = (LEFT, RIGHT)[color]
            for part in range(4):
                piece = own2[t, color, part * PIECE : part * PIECE + PIECE, :]
                own3[t, part, :, lanes] = piece
                send3[t, part, :, lanes] = piece.astype(BF16)
        for k in (2, 1, 3):
            last_copy(t, k).start()

    def finish(t, result):
        for k in (1, 2, 3):
            last_copy(t, k).wait_recv()
        total = own3[t, z]
        for k in range(3):
            total = total + recv3[t, k].astype(F32)
        total = total * scale
        result[pl.ds(0, PIECE, stride=2), :] = total[:, LEFT]
        result[pl.ds(1, PIECE, stride=2), :] = total[:, RIGHT]

    def out_copy(r):
        return pltpu.make_async_copy(stage[r], out.at[0, r - 1], out_sem.at[r - 1])

    def last(*rows):
        def keep(total):
            for k, r in enumerate(rows):
                stage[r][...] = (gv[r][...].astype(F32) + total[span(k), :] * slope[r][...]).astype(BF16)
                out_copy(r).start()

        return conv(h3, lambda a, b: wt1[a, b * CHANS : (b + 1) * CHANS, :], rows, True, keep)

    for pair in loads[:4]:
        for copy in pair:
            copy.wait()
    weights[1].wait()
    weave(turn(wv2, wt2), cots(1, 2, 3, 4))
    pl.semaphore_wait(barrier, len(peers))

    @pl.when(row < 7)
    def _():
        for copy in halos_down:
            copy.start()

    @pl.when(row > 0)
    def _():
        for copy in halos_up:
            copy.start()

    weave(both(backward(2), backward(3)), acted(1, 2, 3, 4))
    weights[0].wait()
    for pair in loads[4:]:
        for copy in pair:
            copy.wait()
    weave(both(forward(2), forward(3)), cots(5, 6, 7, 8) + acted(5, 6))
    weave(both(forward(4, 5), backward(4, 5)), acted(7, 8) + elem(2))
    weave(both(forward(6, 7), backward(6, 7)), elem(3, 4, 5), turn(wv1, wt1))
    weave(one_grads(True, (2, 3), (4, 5)), elem(6, 7))

    @pl.when(row > 0)
    def _():
        for copy in halos_down:
            copy.wait_recv()

    @pl.when(row == 0)
    def _():
        fv[0][...] = jnp.zeros((COLS, CHANS), BF16)
        gv[0][...] = jnp.zeros((COLS, CHANS), BF16)

    @pl.when(row < 7)
    def _():
        for copy in halos_up:
            copy.wait_recv()

    @pl.when(row == 7)
    def _():
        fv[ROWS + 1][...] = jnp.zeros((COLS, CHANS), BF16)
        gv[ROWS + 1][...] = jnp.zeros((COLS, CHANS), BF16)

    weave(one_grads(False, (6, 7)), cots(0, ROWS + 1) + acted(0, ROWS + 1))
    weave(both(forward(1, ROWS), backward(1, ROWS)), grade(1, 2, 3, 4, 5))
    weave(two_grads(True, (4, 5)), elem(1, ROWS))
    hsend[0] = h3[1][:, CHANS : 2 * CHANS]
    hsend[1] = h3[ROWS][:, CHANS : 2 * CHANS]

    @pl.when(row < 7)
    def _():
        h_down.start()

    @pl.when(row > 0)
    def _():
        h_up.start()

    weave(one_grads(False, (1, ROWS)), grade(6, 7, 8))
    core_start(0, range(8))
    inner = two_grads(False, (2, 3), (6, 7))
    weave(inner[:4])
    weave(inner[4:], [functools.partial(core_add, 0, g) for g in range(8)])
    start1(0)
    weave(two_edge(0, (ROWS - 1, ROWS), (ROWS, ROWS + 1)))
    core_start(1, (0, 1))
    weave(two_edge(1, (1, ROWS), (1, ROWS)))
    core_start(1, (2, 3, 4))
    weave(two_edge(2, (2, 1), (1, 0)))
    core_start(1, (5, 6, 7))
    inner = both(last(2, 3), last(4, 5))
    weave(inner[:5], [functools.partial(core_add, 1, g) for g in range(5)])
    for g in (5, 6, 7):
        core_add(1, g)
    start1(1)
    weave(inner[5:])

    @pl.when(row > 0)
    def _():
        h_down.wait_recv()

    @pl.when(row == 0)
    def _():
        hrecv[0] = jnp.zeros((COLS, CHANS), BF16)

    @pl.when(row < 7)
    def _():
        h_up.wait_recv()

    @pl.when(row == 7)
    def _():
        hrecv[1] = jnp.zeros((COLS, CHANS), BF16)

    weave(single(halo_one, 0, ROWS + 1))
    weave(both(last(6, 7), last(1, ROWS)))
    start2(0)
    start2(1)
    start3(0)
    start3(1)
    finish(0, out_one)
    finish(1, out_two)

    @pl.when(row < 7)
    def _():
        for copy in halos_down + [h_down]:
            copy.wait_send()

    @pl.when(row > 0)
    def _():
        for copy in halos_up + [h_up]:
            copy.wait_send()

    for r in range(ROWS):
        out_copy(r + 1).wait()
    for t in range(2):
        for g in range(8):
            core_copy(t, g).wait_send()
        for k in (1, 2, 3):
            for color in range(2):
                for step in range(2):
                    wide_copy(t, color, step, k).wait_send()
            last_copy(t, k).wait_send()


def shards(features, cotangent, weight_one, weight_two):
    height = features.shape[1] * lax.axis_size("row")
    scale = 1.0 / math.sqrt(lax.axis_size("img") * height * features.shape[2])
    hbm = pl.BlockSpec(memory_space=pl.ANY)
    vmem = pl.BlockSpec(memory_space=pltpu.VMEM)
    dma = pltpu.SemaphoreType.DMA
    wide = ROWS + 2
    grad, one, two = pl.pallas_call(
        functools.partial(kernel, scale),
        out_shape=(
            jax.ShapeDtypeStruct(features.shape, BF16),
            jax.ShapeDtypeStruct((2 * PIECE, 128), F32),
            jax.ShapeDtypeStruct((2 * PIECE, 128), F32),
        ),
        in_specs=[hbm] * 4,
        out_specs=(hbm, vmem, vmem),
        scratch_shapes=[
            [pltpu.VMEM((COLS, CHANS), BF16)] * wide,
            [pltpu.VMEM((COLS, CHANS), BF16)] * wide,
            pltpu.VMEM((3, 3, CHANS, CHANS), BF16),
            pltpu.VMEM((3, 3, CHANS, CHANS), BF16),
            pltpu.VMEM((3, WIDE, CHANS), BF16),
            pltpu.VMEM((3, WIDE, CHANS), BF16),
            [pltpu.VMEM((COLS, WIDE), BF16)] * wide,
            [pltpu.VMEM((COLS, WIDE), BF16)] * wide,
            [pltpu.VMEM((COLS, WIDE), BF16)] * wide,
            [pltpu.VMEM((CHANS, COLS), BF16)] * wide,
            [pltpu.VMEM((CHANS, COLS), BF16)] * wide,
            [pltpu.VMEM((COLS, CHANS), F32)] * wide,
            [pltpu.VMEM((COLS, CHANS), F32)] * wide,
            [pltpu.VMEM((COLS, CHANS), F32)] * wide,
            pltpu.VMEM((2, COLS, CHANS), BF16),
            pltpu.VMEM((2, COLS, CHANS), BF16),
            [pltpu.VMEM((COLS, CHANS), BF16)] * wide,
            pltpu.VMEM((2, 9 * CHANS, CHANS), F32),
            pltpu.VMEM((2, 8, GROUP, CHANS), F32),
            pltpu.VMEM((2, 2, 4, 2 * GROUP, 128), BF16),
            pltpu.VMEM((2, 2, 3, 2 * GROUP, 128), BF16),
            pltpu.VMEM((2, 2, 4, GROUP // 2, 128), F32),
            pltpu.VMEM((2, 2, 4, GROUP // 2, 128), BF16),
            pltpu.VMEM((2, 2, 3, GROUP // 2, 128), BF16),
            pltpu.VMEM((2, 2, GROUP // 2, 128), F32),
            pltpu.VMEM((2, 4, PIECE, CHANS), BF16),
            pltpu.VMEM((2, 3, PIECE, CHANS), BF16),
            pltpu.VMEM((2, 4, PIECE, CHANS), F32),
            dma((2, ROWS)),
            dma((2,)),
            dma((3, 2)),
            dma((3, 2)),
            dma((ROWS,)),
            dma((2, 8)),
            dma((2, 8)),
            dma((2, 2, 2, 3)),
            dma((2, 2, 2, 3)),
            dma((2, 3)),
            dma((2, 3)),
        ],
        compiler_params=pltpu.CompilerParams(
            collective_id=0, has_side_effects=True, vmem_limit_bytes=64 * 1000 * 1000
        ),
        name="unit_backward",
    )(features, cotangent, weight_one, weight_two)
    return grad, one.reshape(-1), two.reshape(-1)


def solution(mesh):
    placed = (P("img", "row", None, None), P("img", "row", None, None), P(), P())
    return jax.shard_map(
        shards,
        mesh=mesh,
        in_specs=placed,
        out_specs=(P("img", "row", None, None), P(("img", "row")), P(("img", "row"))),
        check_vma=False,
    )
```

```python
import functools
import math

import jax
import jax.numpy as jnp
from jax import lax
from jax.experimental import pallas as pl
from jax.experimental.pallas import tpu as pltpu
from jax.sharding import PartitionSpec as P

MESH = pl.DeviceIdType.MESH
F32 = jnp.float32
BF16 = jnp.bfloat16
COEFF = 0.7978845608028654
CUBIC = 0.044715
ROWS = 8
COLS = 384
CHANS = 256
WIDE = 3 * CHANS
CELLS = ROWS * COLS
GROUP = 144
PIECE = 18


def gelu_terms(v):
    poly = COEFF + (COEFF * CUBIC) * (v * v)
    half = 0.5 + 0.5 * jnp.tanh(v * poly)
    return v * half, half, poly


def slope_of(acted, half, poly):
    return half + acted * (1.0 - half) * (6.0 * poly - 4.0 * COEFF)


def span(row, count=1):
    return slice(row * COLS, (row + count) * COLS)


def rows_of(refs, rows, columns):
    return jnp.concatenate([refs[r][:, columns] for r in rows], axis=0)


def lanes_of(refs, rows):
    return jnp.concatenate([refs[r][...] for r in rows], axis=1)


def weave(*streams):
    longest = max(len(stream) for stream in streams)
    done = [0] * len(streams)
    for step in range(longest):
        for k, stream in enumerate(streams):
            end = (step + 1) * len(stream) // longest
            for task in stream[done[k] : end]:
                task()
            done[k] = end


def kernel(
    scale,
    feat,
    cot,
    w_one,
    w_two,
    out,
    out_one,
    out_two,
    fv,
    gv,
    wv1,
    wv2,
    wt1,
    wt2,
    a3,
    g3,
    h3,
    at,
    gt,
    slope,
    hid,
    bh,
    hsend,
    hrecv,
    stage,
    acc,
    crecv,
    send1,
    recv1,
    own1,
    send2,
    recv2,
    own2,
    send3,
    recv3,
    own3,
    load_sem,
    w_sem,
    halo_send,
    halo_recv,
    out_sem,
    core_send,
    core_recv,
    wide_send,
    wide_recv,
    last_send,
    last_recv,
):
    img, row = lax.axis_index("img"), lax.axis_index("row")
    core, y_lo, x = img % 2, (img // 2) % 2, img // 4
    z, y_hi = row % 4, row // 4
    y = y_hi * 2 + y_lo

    def x_peer(k):
        there = (x + k) % 4
        return there, ((there * 2 + y_lo) * 2 + core, row)

    def y_peer(k):
        there = (y + k) % 4
        return there, ((x * 2 + there % 2) * 2 + core, (there // 2) * 4 + z)

    def z_peer(k):
        there = (z + k) % 4
        return there, (img, y_hi * 4 + there)

    partner = ((x * 2 + y_lo) * 2 + (1 - core), row)
    below, above = (img, (row + 1) % 8), (img, (row + 7) % 8)

    loads = [
        (
            pltpu.make_async_copy(feat.at[0, r], fv[r + 1], load_sem.at[0, r]),
            pltpu.make_async_copy(cot.at[0, r], gv[r + 1], load_sem.at[1, r]),
        )
        for r in range(ROWS)
    ]
    weights = [
        pltpu.make_async_copy(w_one, wv1, w_sem.at[0]),
        pltpu.make_async_copy(w_two, wv2, w_sem.at[1]),
    ]
    for pair in loads[:4]:
        for copy in pair:
            copy.start()
    for copy in weights:
        copy.start()
    for pair in loads[4:]:
        for copy in pair:
            copy.start()

    barrier = pltpu.get_barrier_semaphore()
    peers = [partner, below, above]
    for peer in (x_peer, y_peer, z_peer):
        for k in (1, 2, 3):
            peers.append(peer(k)[1])
    for peer in peers:
        pl.semaphore_signal(barrier, inc=1, device_id=peer, device_id_type=MESH)

    def halo(which, down, src, dst):
        return pltpu.make_async_remote_copy(
            src_ref=src,
            dst_ref=dst,
            send_sem=halo_send.at[which, down],
            recv_sem=halo_recv.at[which, down],
            device_id=below if down else above,
            device_id_type=MESH,
        )

    halos_down = [
        halo(0, 1, feat.at[0, ROWS - 1], fv[0]),
        halo(1, 1, cot.at[0, ROWS - 1], gv[0]),
    ]
    halos_up = [
        halo(0, 0, feat.at[0, 0], fv[ROWS + 1]),
        halo(1, 0, cot.at[0, 0], gv[ROWS + 1]),
    ]
    h_down = halo(2, 1, hsend.at[1], hrecv.at[0])
    h_up = halo(2, 0, hsend.at[0], hrecv.at[1])

    def turn(source, target):
        def block(a, b):
            target[a, b * CHANS : (b + 1) * CHANS, :] = source[a, b].T

        return [functools.partial(block, a, b) for a in range(3) for b in range(3)]

    def window(ref, lane, c):
        blank = jnp.zeros((8, 128), F32)
        low, high = 128 * c - 8, 128 * c + 136
        inside = ref[max(low, 0) : min(high, COLS), lane : lane + 128].astype(F32)
        if c == 0:
            inside = jnp.concatenate([blank, inside], axis=0)
        if c == 2:
            inside = jnp.concatenate([inside, blank], axis=0)
        return pltpu.roll(inside, 1, 0)[8:136], pltpu.roll(inside, 143, 0)[8:136]

    def block(lane, c):
        return slice(128 * c, 128 * c + 128), slice(lane, lane + 128)

    def wide_block(lane, c, tap):
        return slice(128 * c, 128 * c + 128), slice(tap * CHANS + lane, tap * CHANS + lane + 128)

    def acted_one(r, lane, c):
        acted, _, _ = gelu_terms(fv[r][block(lane, c)].astype(F32))
        mid = acted.astype(BF16)
        hid[r][block(lane, c)] = acted
        a3[r][wide_block(lane, c, 1)] = mid
        at[r][lane : lane + 128, 128 * c : 128 * c + 128] = mid.T

    def acted_two(r, lane, c):
        left, right = window(hid[r], lane, c)
        a3[r][wide_block(lane, c, 0)] = left.astype(BF16)
        a3[r][wide_block(lane, c, 2)] = right.astype(BF16)

    def cot_one(r, lane, c):
        left, right = window(gv[r], lane, c)
        g3[r][wide_block(lane, c, 0)] = right.astype(BF16)
        g3[r][wide_block(lane, c, 1)] = gv[r][block(lane, c)]
        g3[r][wide_block(lane, c, 2)] = left.astype(BF16)

    def grade_one(r, lane, c):
        slope[r][block(lane, c)] = slope_of(*gelu_terms(fv[r][block(lane, c)].astype(F32)))

    def elem_one(r, lane, c):
        terms = gelu_terms(hid[r][block(lane, c)])
        gt[r][lane : lane + 128, 128 * c : 128 * c + 128] = terms[0].astype(BF16).T
        grad = bh[r][block(lane, c)] * slope_of(*terms)
        bh[r][block(lane, c)] = grad
        h3[r][wide_block(lane, c, 1)] = grad.astype(BF16)

    def elem_two(r, lane, c):
        left, right = window(bh[r], lane, c)
        h3[r][wide_block(lane, c, 0)] = right.astype(BF16)
        h3[r][wide_block(lane, c, 2)] = left.astype(BF16)

    def halo_one(r, lane, c):
        left, right = window(hrecv.at[r // ROWS], lane, c)
        h3[r][wide_block(lane, c, 0)] = right.astype(BF16)
        h3[r][wide_block(lane, c, 1)] = hrecv[r // ROWS, 128 * c : 128 * c + 128, lane : lane + 128]
        h3[r][wide_block(lane, c, 2)] = left.astype(BF16)

    def single(task, *rows):
        return [functools.partial(task, r, lane, c) for r in rows for lane in (0, 128) for c in range(3)]

    def double(one, two, *rows):
        order = ((one, 0), (one, 1), (two, 0), (one, 2), (two, 1), (two, 2))
        return [functools.partial(f, r, lane, c) for r in rows for lane in (0, 128) for f, c in order]

    def acted(*rows):
        return double(acted_one, acted_two, *rows)

    def elem(*rows):
        return double(elem_one, elem_two, *rows)

    def cots(*rows):
        return single(cot_one, *rows)

    def grade(*rows):
        return single(grade_one, *rows)

    def both(*streams):
        def step(tasks):
            for task in tasks:
                task()

        return [functools.partial(step, tasks) for tasks in zip(*streams, strict=True)]

    def conv(source, weight, rows, flip, keep):
        box = [None]

        def step(a, b):
            near = [r - a + 1 if flip else r + a - 1 for r in rows]
            columns = slice(b * CHANS, (b + 1) * CHANS)
            part = jnp.dot(rows_of(source, near, columns), weight(a, b), preferred_element_type=F32)
            box[0] = part if box[0] is None else box[0] + part
            if (a, b) == (2, 2):
                keep(box[0])

        return [functools.partial(step, a, b) for a in range(3) for b in range(3)]

    def keep_in(refs, rows):
        def keep(total):
            for k, r in enumerate(rows):
                refs[r][...] = total[span(k), :]

        return keep

    def forward(*rows):
        return conv(a3, lambda a, b: wv1[a, b], rows, False, keep_in(hid, rows))

    def backward(*rows):
        return conv(
            g3, lambda a, b: wt2[a, b * CHANS : (b + 1) * CHANS, :], rows, True, keep_in(bh, rows)
        )

    def grads(t, fresh, terms, taps=(0, 1, 2)):
        tall = len(taps) * CHANS

        def build(b, low, high):
            box = [None]

            def step(pair, part, final):
                lhs = jnp.concatenate([lanes_of(*pair[k]) for k in range(len(taps))], axis=0)[low:high]
                rhs = rows_of(pair[-1][0], pair[-1][1], slice(b * CHANS, (b + 1) * CHANS))
                deep = slice(part * CHANS, (part + 1) * CHANS)
                product = jnp.dot(lhs[:, deep], rhs[deep, :], preferred_element_type=F32)
                box[0] = product if box[0] is None else box[0] + product
                if final:
                    for k, a in enumerate(taps):
                        start, end = max(low, k * CHANS), min(high, (k + 1) * CHANS)
                        if start < end:
                            base = (a * 3 + b) * CHANS - k * CHANS
                            here = slice(base + start, base + end)
                            piece = box[0][start - low : end - low, :]
                            acc[t, here, :] = piece if fresh else acc[t, here, :] + piece

            return [
                functools.partial(step, pair, part, pair is terms[-1] and part == 2)
                for pair in terms
                for part in range(3)
            ]

        half = tall // 2
        return both(build(0, 0, tall), build(1, 0, tall)) + both(build(2, 0, half), build(2, half, tall))

    def one_grads(fresh, *pairs):
        terms = [[(at, (p + a - 1, q + a - 1)) for a in range(3)] + [(h3, (p, q))] for p, q in pairs]
        return grads(0, fresh, terms)

    def two_grads(fresh, *pairs):
        terms = [[(gt, (p + a - 1, q + a - 1)) for a in range(3)] + [(g3, (p, q))] for p, q in pairs]
        return grads(1, fresh, terms)

    def two_edge(a, left, right):
        return grads(1, False, [[(gt, left), (g3, right)]], (a,))

    def core_copy(t, g):
        return pltpu.make_async_remote_copy(
            src_ref=acc.at[t, pl.ds(pl.multiple_of((2 * g + 1 - core) * GROUP, GROUP), GROUP)],
            dst_ref=crecv.at[t, g],
            send_sem=core_send.at[t, g],
            recv_sem=core_recv.at[t, g],
            device_id=partner,
            device_id_type=MESH,
        )

    def wide_copy(t, color, step, k):
        send, recv = ((send1, recv1), (send2, recv2))[step]
        there, device = (x_peer if color == step else y_peer)(k)
        return pltpu.make_async_remote_copy(
            src_ref=send.at[t, color, there],
            dst_ref=recv.at[t, color, k - 1],
            send_sem=wide_send.at[t, color, step, k - 1],
            recv_sem=wide_recv.at[t, color, step, k - 1],
            device_id=device,
            device_id_type=MESH,
        )

    def last_copy(t, k):
        there, device = z_peer(k)
        return pltpu.make_async_remote_copy(
            src_ref=send3.at[t, there],
            dst_ref=recv3.at[t, k - 1],
            send_sem=last_send.at[t, k - 1],
            recv_sem=last_recv.at[t, k - 1],
            device_id=device,
            device_id_type=MESH,
        )

    HALF = GROUP // 2
    LEFT, RIGHT = slice(0, 128), slice(128, 256)

    def core_start(t, groups):
        for g in groups:
            core_copy(t, g).start()

    def core_add(t, g):
        core_copy(t, g).wait_recv()
        here = pl.ds(pl.multiple_of((2 * g + core) * GROUP, GROUP), GROUP)
        total = acc[t, here, :] + crecv[t, g]
        crecv[t, g] = total
        place, low = g // 2, g % 2
        send1[t, 0, place, low * GROUP : (low + 1) * GROUP, :] = total[:, LEFT].astype(BF16)
        for high in range(2):
            send1[t, 1, high * 2 + low, place * HALF : (place + 1) * HALF, :] = total[
                high * HALF : (high + 1) * HALF, RIGHT
            ].astype(BF16)

    def start1(t):
        for k in (2, 1, 3):
            for color in range(2):
                wide_copy(t, color, 0, k).start()

    def start2(t):
        for color in range(2):
            for k in (1, 2, 3):
                wide_copy(t, color, 0, k).wait_recv()
        for low in range(2):
            for high in range(2):
                rows = slice(low * GROUP + high * HALF, low * GROUP + (high + 1) * HALF)
                total = crecv[t, 2 * x + low, high * HALF : (high + 1) * HALF, LEFT]
                for k in range(3):
                    total = total + recv1[t, 0, k, rows, :].astype(F32)
                own1[t, 0, high * 2 + low] = total
                send2[t, 0, high * 2 + low] = total.astype(BF16)
        for place in range(4):
            rows = slice(place * HALF, (place + 1) * HALF)
            total = crecv[t, 2 * place + y_lo, pl.ds(pl.multiple_of(y_hi * HALF, HALF), HALF), RIGHT]
            for k in range(3):
                total = total + recv1[t, 1, k, rows, :].astype(F32)
            own1[t, 1, place] = total
            send2[t, 1, place] = total.astype(BF16)
        for k in (2, 1, 3):
            for color in range(2):
                wide_copy(t, color, 1, k).start()

    def start3(t):
        for color, mine in ((0, y), (1, x)):
            for k in (1, 2, 3):
                wide_copy(t, color, 1, k).wait_recv()
            total = own1[t, color, mine]
            for k in range(3):
                total = total + recv2[t, color, k].astype(F32)
            own2[t, color] = total
            lanes = (LEFT, RIGHT)[color]
            for part in range(4):
                piece = own2[t, color, part * PIECE : part * PIECE + PIECE, :]
                own3[t, part, :, lanes] = piece
                send3[t, part, :, lanes] = piece.astype(BF16)
        for k in (2, 1, 3):
            last_copy(t, k).start()

    def finish(t, result):
        for k in (1, 2, 3):
            last_copy(t, k).wait_recv()
        total = own3[t, z]
        for k in range(3):
            total = total + recv3[t, k].astype(F32)
        total = total * scale
        result[pl.ds(0, PIECE, stride=2), :] = total[:, LEFT]
        result[pl.ds(1, PIECE, stride=2), :] = total[:, RIGHT]

    def out_copy(r):
        return pltpu.make_async_copy(stage[r], out.at[0, r - 1], out_sem.at[r - 1])

    def last(*rows):
        def keep(total):
            for k, r in enumerate(rows):
                stage[r][...] = (gv[r][...].astype(F32) + total[span(k), :] * slope[r][...]).astype(BF16)
                out_copy(r).start()

        return conv(h3, lambda a, b: wt1[a, b * CHANS : (b + 1) * CHANS, :], rows, True, keep)

    for pair in loads[:4]:
        for copy in pair:
            copy.wait()
    weights[1].wait()
    weave(turn(wv2, wt2), cots(1, 2, 3, 4))
    pl.semaphore_wait(barrier, len(peers))

    @pl.when(row < 7)
    def _():
        for copy in halos_down:
            copy.start()

    @pl.when(row > 0)
    def _():
        for copy in halos_up:
            copy.start()

    weave(both(backward(2), backward(3)), acted(1, 2, 3, 4))
    weights[0].wait()
    for pair in loads[4:]:
        for copy in pair:
            copy.wait()
    weave(both(forward(2), forward(3)), cots(5, 6, 7, 8) + acted(5, 6))
    weave(both(forward(4, 5), backward(4, 5)), acted(7, 8) + elem(2))
    weave(both(forward(6, 7), backward(6, 7)), elem(3, 4, 5), turn(wv1, wt1))
    weave(one_grads(True, (2, 3), (4, 5)), elem(6, 7))

    @pl.when(row > 0)
    def _():
        for copy in halos_down:
            copy.wait_recv()

    @pl.when(row == 0)
    def _():
        fv[0][...] = jnp.zeros((COLS, CHANS), BF16)
        gv[0][...] = jnp.zeros((COLS, CHANS), BF16)

    @pl.when(row < 7)
    def _():
        for copy in halos_up:
            copy.wait_recv()

    @pl.when(row == 7)
    def _():
        fv[ROWS + 1][...] = jnp.zeros((COLS, CHANS), BF16)
        gv[ROWS + 1][...] = jnp.zeros((COLS, CHANS), BF16)

    weave(one_grads(False, (6, 7)), cots(0, ROWS + 1) + acted(0, ROWS + 1))
    weave(both(forward(1, ROWS), backward(1, ROWS)))
    weave(two_grads(True, (4, 5)), elem(1, ROWS))
    hsend[0] = h3[1][:, CHANS : 2 * CHANS]
    hsend[1] = h3[ROWS][:, CHANS : 2 * CHANS]

    @pl.when(row < 7)
    def _():
        h_down.start()

    @pl.when(row > 0)
    def _():
        h_up.start()

    weave(one_grads(False, (1, ROWS)))
    core_start(0, range(8))
    inner = two_grads(False, (2, 3), (6, 7))
    weave(inner[:4])
    weave(inner[4:], [functools.partial(core_add, 0, g) for g in range(8)])
    start1(0)
    weave(two_edge(0, (ROWS - 1, ROWS), (ROWS, ROWS + 1)))
    core_start(1, (0, 1))
    weave(two_edge(1, (1, ROWS), (1, ROWS)))
    core_start(1, (2, 3, 4))
    weave(two_edge(2, (2, 1), (1, 0)))
    core_start(1, (5, 6, 7))
    inner = both(last(2, 3), last(4, 5))
    weave(inner[:5], [functools.partial(core_add, 1, g) for g in range(5)])
    for g in (5, 6, 7):
        core_add(1, g)
    start1(1)
    weave(inner[5:8], grade(2, 3, 4, 5))
    weave(inner[8:])

    @pl.when(row > 0)
    def _():
        h_down.wait_recv()

    @pl.when(row == 0)
    def _():
        hrecv[0] = jnp.zeros((COLS, CHANS), BF16)

    @pl.when(row < 7)
    def _():
        h_up.wait_recv()

    @pl.when(row == 7)
    def _():
        hrecv[1] = jnp.zeros((COLS, CHANS), BF16)

    weave(single(halo_one, 0, ROWS + 1))
    inner = both(last(6, 7), last(1, ROWS))
    weave(inner[:8], grade(6, 7, 1, ROWS))
    weave(inner[8:])
    start2(0)
    start2(1)
    start3(0)
    start3(1)
    finish(0, out_one)
    finish(1, out_two)

    @pl.when(row < 7)
    def _():
        for copy in halos_down + [h_down]:
            copy.wait_send()

    @pl.when(row > 0)
    def _():
        for copy in halos_up + [h_up]:
            copy.wait_send()

    for r in range(ROWS):
        out_copy(r + 1).wait()
    for t in range(2):
        for g in range(8):
            core_copy(t, g).wait_send()
        for k in (1, 2, 3):
            for color in range(2):
                for step in range(2):
                    wide_copy(t, color, step, k).wait_send()
            last_copy(t, k).wait_send()


def shards(features, cotangent, weight_one, weight_two):
    height = features.shape[1] * lax.axis_size("row")
    scale = 1.0 / math.sqrt(lax.axis_size("img") * height * features.shape[2])
    hbm = pl.BlockSpec(memory_space=pl.ANY)
    vmem = pl.BlockSpec(memory_space=pltpu.VMEM)
    dma = pltpu.SemaphoreType.DMA
    wide = ROWS + 2
    grad, one, two = pl.pallas_call(
        functools.partial(kernel, scale),
        out_shape=(
            jax.ShapeDtypeStruct(features.shape, BF16),
            jax.ShapeDtypeStruct((2 * PIECE, 128), F32),
            jax.ShapeDtypeStruct((2 * PIECE, 128), F32),
        ),
        in_specs=[hbm] * 4,
        out_specs=(hbm, vmem, vmem),
        scratch_shapes=[
            [pltpu.VMEM((COLS, CHANS), BF16)] * wide,
            [pltpu.VMEM((COLS, CHANS), BF16)] * wide,
            pltpu.VMEM((3, 3, CHANS, CHANS), BF16),
            pltpu.VMEM((3, 3, CHANS, CHANS), BF16),
            pltpu.VMEM((3, WIDE, CHANS), BF16),
            pltpu.VMEM((3, WIDE, CHANS), BF16),
            [pltpu.VMEM((COLS, WIDE), BF16)] * wide,
            [pltpu.VMEM((COLS, WIDE), BF16)] * wide,
            [pltpu.VMEM((COLS, WIDE), BF16)] * wide,
            [pltpu.VMEM((CHANS, COLS), BF16)] * wide,
            [pltpu.VMEM((CHANS, COLS), BF16)] * wide,
            [pltpu.VMEM((COLS, CHANS), F32)] * wide,
            [pltpu.VMEM((COLS, CHANS), F32)] * wide,
            [pltpu.VMEM((COLS, CHANS), F32)] * wide,
            pltpu.VMEM((2, COLS, CHANS), BF16),
            pltpu.VMEM((2, COLS, CHANS), BF16),
            [pltpu.VMEM((COLS, CHANS), BF16)] * wide,
            pltpu.VMEM((2, 9 * CHANS, CHANS), F32),
            pltpu.VMEM((2, 8, GROUP, CHANS), F32),
            pltpu.VMEM((2, 2, 4, 2 * GROUP, 128), BF16),
            pltpu.VMEM((2, 2, 3, 2 * GROUP, 128), BF16),
            pltpu.VMEM((2, 2, 4, GROUP // 2, 128), F32),
            pltpu.VMEM((2, 2, 4, GROUP // 2, 128), BF16),
            pltpu.VMEM((2, 2, 3, GROUP // 2, 128), BF16),
            pltpu.VMEM((2, 2, GROUP // 2, 128), F32),
            pltpu.VMEM((2, 4, PIECE, CHANS), BF16),
            pltpu.VMEM((2, 3, PIECE, CHANS), BF16),
            pltpu.VMEM((2, 4, PIECE, CHANS), F32),
            dma((2, ROWS)),
            dma((2,)),
            dma((3, 2)),
            dma((3, 2)),
            dma((ROWS,)),
            dma((2, 8)),
            dma((2, 8)),
            dma((2, 2, 2, 3)),
            dma((2, 2, 2, 3)),
            dma((2, 3)),
            dma((2, 3)),
        ],
        compiler_params=pltpu.CompilerParams(
            collective_id=0, has_side_effects=True, vmem_limit_bytes=64 * 1000 * 1000
        ),
        name="unit_backward",
    )(features, cotangent, weight_one, weight_two)
    return grad, one.reshape(-1), two.reshape(-1)


def solution(mesh):
    placed = (P("img", "row", None, None), P("img", "row", None, None), P(), P())
    return jax.shard_map(
        shards,
        mesh=mesh,
        in_specs=placed,
        out_specs=(P("img", "row", None, None), P(("img", "row")), P(("img", "row"))),
        check_vma=False,
    )
```

```python
import functools
import math

import jax
import jax.numpy as jnp
from jax import lax
from jax.experimental import pallas as pl
from jax.experimental.pallas import tpu as pltpu
from jax.sharding import PartitionSpec as P

MESH = pl.DeviceIdType.MESH
F32 = jnp.float32
BF16 = jnp.bfloat16
COEFF = 0.7978845608028654
CUBIC = 0.044715
ROWS = 8
COLS = 384
CHANS = 256
WIDE = 3 * CHANS
CELLS = ROWS * COLS
GROUP = 144
PIECE = 18


def gelu_terms(v):
    poly = COEFF + (COEFF * CUBIC) * (v * v)
    half = 0.5 + 0.5 * jnp.tanh(v * poly)
    return v * half, half, poly


def slope_of(acted, half, poly):
    return half + acted * (1.0 - half) * (6.0 * poly - 4.0 * COEFF)


def span(row, count=1):
    return slice(row * COLS, (row + count) * COLS)


def rows_of(refs, rows, columns):
    return jnp.concatenate([refs[r][:, columns] for r in rows], axis=0)


def lanes_of(refs, rows):
    return jnp.concatenate([refs[r][...] for r in rows], axis=1)


def weave(*streams):
    longest = max(len(stream) for stream in streams)
    done = [0] * len(streams)
    for step in range(longest):
        for k, stream in enumerate(streams):
            end = (step + 1) * len(stream) // longest
            for task in stream[done[k] : end]:
                task()
            done[k] = end


def kernel(
    scale,
    feat,
    cot,
    w_one,
    w_two,
    out,
    out_one,
    out_two,
    fv,
    gv,
    wv1,
    wv2,
    wt1,
    wt2,
    a3,
    g3,
    h3,
    at,
    gt,
    slope,
    hid,
    bh,
    hsend,
    hrecv,
    stage,
    acc,
    crecv,
    send1,
    recv1,
    own1,
    send2,
    recv2,
    own2,
    send3,
    recv3,
    own3,
    load_sem,
    w_sem,
    halo_send,
    halo_recv,
    out_sem,
    core_send,
    core_recv,
    wide_send,
    wide_recv,
    last_send,
    last_recv,
):
    img, row = lax.axis_index("img"), lax.axis_index("row")
    core, y_lo, x = img % 2, (img // 2) % 2, img // 4
    z, y_hi = row % 4, row // 4
    y = y_hi * 2 + y_lo

    def x_peer(k):
        there = (x + k) % 4
        return there, ((there * 2 + y_lo) * 2 + core, row)

    def y_peer(k):
        there = (y + k) % 4
        return there, ((x * 2 + there % 2) * 2 + core, (there // 2) * 4 + z)

    def z_peer(k):
        there = (z + k) % 4
        return there, (img, y_hi * 4 + there)

    partner = ((x * 2 + y_lo) * 2 + (1 - core), row)
    below, above = (img, (row + 1) % 8), (img, (row + 7) % 8)

    loads = [
        (
            pltpu.make_async_copy(feat.at[0, r], fv[r + 1], load_sem.at[0, r]),
            pltpu.make_async_copy(cot.at[0, r], gv[r + 1], load_sem.at[1, r]),
        )
        for r in range(ROWS)
    ]
    weights = [
        pltpu.make_async_copy(w_one, wv1, w_sem.at[0]),
        pltpu.make_async_copy(w_two, wv2, w_sem.at[1]),
    ]
    for r in range(4):
        loads[r][1].start()
    weights[1].start()
    for r in range(4):
        loads[r][0].start()
    weights[0].start()
    for pair in loads[4:]:
        for copy in reversed(pair):
            copy.start()

    barrier = pltpu.get_barrier_semaphore()
    peers = [partner, below, above]
    for peer in (x_peer, y_peer, z_peer):
        for k in (1, 2, 3):
            peers.append(peer(k)[1])
    for peer in peers:
        pl.semaphore_signal(barrier, inc=1, device_id=peer, device_id_type=MESH)

    def halo(which, down, src, dst):
        return pltpu.make_async_remote_copy(
            src_ref=src,
            dst_ref=dst,
            send_sem=halo_send.at[which, down],
            recv_sem=halo_recv.at[which, down],
            device_id=below if down else above,
            device_id_type=MESH,
        )

    halos_down = [
        halo(0, 1, feat.at[0, ROWS - 1], fv[0]),
        halo(1, 1, cot.at[0, ROWS - 1], gv[0]),
    ]
    halos_up = [
        halo(0, 0, feat.at[0, 0], fv[ROWS + 1]),
        halo(1, 0, cot.at[0, 0], gv[ROWS + 1]),
    ]
    h_down = halo(2, 1, hsend.at[1], hrecv.at[0])
    h_up = halo(2, 0, hsend.at[0], hrecv.at[1])

    def turn(source, target):
        def block(a, b):
            target[a, b * CHANS : (b + 1) * CHANS, :] = source[a, b].T

        return [functools.partial(block, a, b) for a in range(3) for b in range(3)]

    def window(ref, lane, c):
        blank = jnp.zeros((8, 128), F32)
        low, high = 128 * c - 8, 128 * c + 136
        inside = ref[max(low, 0) : min(high, COLS), lane : lane + 128].astype(F32)
        if c == 0:
            inside = jnp.concatenate([blank, inside], axis=0)
        if c == 2:
            inside = jnp.concatenate([inside, blank], axis=0)
        return pltpu.roll(inside, 1, 0)[8:136], pltpu.roll(inside, 143, 0)[8:136]

    def block(lane, c):
        return slice(128 * c, 128 * c + 128), slice(lane, lane + 128)

    def wide_block(lane, c, tap):
        return slice(128 * c, 128 * c + 128), slice(tap * CHANS + lane, tap * CHANS + lane + 128)

    def acted_one(r, lane, c):
        acted, _, _ = gelu_terms(fv[r][block(lane, c)].astype(F32))
        mid = acted.astype(BF16)
        hid[r][block(lane, c)] = acted
        a3[r][wide_block(lane, c, 1)] = mid
        at[r][lane : lane + 128, 128 * c : 128 * c + 128] = mid.T

    def acted_two(r, lane, c):
        left, right = window(hid[r], lane, c)
        a3[r][wide_block(lane, c, 0)] = left.astype(BF16)
        a3[r][wide_block(lane, c, 2)] = right.astype(BF16)

    def cot_one(r, lane, c):
        left, right = window(gv[r], lane, c)
        g3[r][wide_block(lane, c, 0)] = right.astype(BF16)
        g3[r][wide_block(lane, c, 1)] = gv[r][block(lane, c)]
        g3[r][wide_block(lane, c, 2)] = left.astype(BF16)

    def grade_one(r, lane, c):
        slope[r][block(lane, c)] = slope_of(*gelu_terms(fv[r][block(lane, c)].astype(F32)))

    def elem_one(r, lane, c):
        terms = gelu_terms(hid[r][block(lane, c)])
        gt[r][lane : lane + 128, 128 * c : 128 * c + 128] = terms[0].astype(BF16).T
        grad = bh[r][block(lane, c)] * slope_of(*terms)
        bh[r][block(lane, c)] = grad
        h3[r][wide_block(lane, c, 1)] = grad.astype(BF16)

    def elem_two(r, lane, c):
        left, right = window(bh[r], lane, c)
        h3[r][wide_block(lane, c, 0)] = right.astype(BF16)
        h3[r][wide_block(lane, c, 2)] = left.astype(BF16)

    def halo_one(r, lane, c):
        left, right = window(hrecv.at[r // ROWS], lane, c)
        h3[r][wide_block(lane, c, 0)] = right.astype(BF16)
        h3[r][wide_block(lane, c, 1)] = hrecv[r // ROWS, 128 * c : 128 * c + 128, lane : lane + 128]
        h3[r][wide_block(lane, c, 2)] = left.astype(BF16)

    def single(task, *rows):
        return [functools.partial(task, r, lane, c) for r in rows for lane in (0, 128) for c in range(3)]

    def double(one, two, *rows):
        order = ((one, 0), (one, 1), (two, 0), (one, 2), (two, 1), (two, 2))
        return [functools.partial(f, r, lane, c) for r in rows for lane in (0, 128) for f, c in order]

    def acted(*rows):
        return double(acted_one, acted_two, *rows)

    def elem(*rows):
        return double(elem_one, elem_two, *rows)

    def cots(*rows):
        return single(cot_one, *rows)

    def grade(*rows):
        return single(grade_one, *rows)

    def both(*streams):
        def step(tasks):
            for task in tasks:
                task()

        return [functools.partial(step, tasks) for tasks in zip(*streams, strict=True)]

    def conv(source, weight, rows, flip, keep):
        box = [None]

        def step(a, b):
            near = [r - a + 1 if flip else r + a - 1 for r in rows]
            columns = slice(b * CHANS, (b + 1) * CHANS)
            part = jnp.dot(rows_of(source, near, columns), weight(a, b), preferred_element_type=F32)
            box[0] = part if box[0] is None else box[0] + part
            if (a, b) == (2, 2):
                keep(box[0])

        return [functools.partial(step, a, b) for a in range(3) for b in range(3)]

    def keep_in(refs, rows):
        def keep(total):
            for k, r in enumerate(rows):
                refs[r][...] = total[span(k), :]

        return keep

    def forward(*rows):
        return conv(a3, lambda a, b: wv1[a, b], rows, False, keep_in(hid, rows))

    def backward(*rows):
        return conv(
            g3, lambda a, b: wt2[a, b * CHANS : (b + 1) * CHANS, :], rows, True, keep_in(bh, rows)
        )

    def grads(t, fresh, terms, taps=(0, 1, 2)):
        tall = len(taps) * CHANS

        def build(b, low, high):
            box = [None]

            def step(pair, part, final):
                lhs = jnp.concatenate([lanes_of(*pair[k]) for k in range(len(taps))], axis=0)[low:high]
                rhs = rows_of(pair[-1][0], pair[-1][1], slice(b * CHANS, (b + 1) * CHANS))
                deep = slice(part * CHANS, (part + 1) * CHANS)
                product = jnp.dot(lhs[:, deep], rhs[deep, :], preferred_element_type=F32)
                box[0] = product if box[0] is None else box[0] + product
                if final:
                    for k, a in enumerate(taps):
                        start, end = max(low, k * CHANS), min(high, (k + 1) * CHANS)
                        if start < end:
                            base = (a * 3 + b) * CHANS - k * CHANS
                            here = slice(base + start, base + end)
                            piece = box[0][start - low : end - low, :]
                            acc[t, here, :] = piece if fresh else acc[t, here, :] + piece

            return [
                functools.partial(step, pair, part, pair is terms[-1] and part == 2)
                for pair in terms
                for part in range(3)
            ]

        half = tall // 2
        return both(build(0, 0, tall), build(1, 0, tall)) + both(build(2, 0, half), build(2, half, tall))

    def one_grads(fresh, *pairs):
        terms = [[(at, (p + a - 1, q + a - 1)) for a in range(3)] + [(h3, (p, q))] for p, q in pairs]
        return grads(0, fresh, terms)

    def two_grads(fresh, *pairs):
        terms = [[(gt, (p + a - 1, q + a - 1)) for a in range(3)] + [(g3, (p, q))] for p, q in pairs]
        return grads(1, fresh, terms)

    def two_edge(a, left, right):
        return grads(1, False, [[(gt, left), (g3, right)]], (a,))

    def core_copy(t, g):
        return pltpu.make_async_remote_copy(
            src_ref=acc.at[t, pl.ds(pl.multiple_of((2 * g + 1 - core) * GROUP, GROUP), GROUP)],
            dst_ref=crecv.at[t, g],
            send_sem=core_send.at[t, g],
            recv_sem=core_recv.at[t, g],
            device_id=partner,
            device_id_type=MESH,
        )

    def wide_copy(t, color, step, k):
        send, recv = ((send1, recv1), (send2, recv2))[step]
        there, device = (x_peer if color == step else y_peer)(k)
        return pltpu.make_async_remote_copy(
            src_ref=send.at[t, color, there],
            dst_ref=recv.at[t, color, k - 1],
            send_sem=wide_send.at[t, color, step, k - 1],
            recv_sem=wide_recv.at[t, color, step, k - 1],
            device_id=device,
            device_id_type=MESH,
        )

    def last_copy(t, k):
        there, device = z_peer(k)
        return pltpu.make_async_remote_copy(
            src_ref=send3.at[t, there],
            dst_ref=recv3.at[t, k - 1],
            send_sem=last_send.at[t, k - 1],
            recv_sem=last_recv.at[t, k - 1],
            device_id=device,
            device_id_type=MESH,
        )

    HALF = GROUP // 2
    LEFT, RIGHT = slice(0, 128), slice(128, 256)

    def core_start(t, groups):
        for g in groups:
            core_copy(t, g).start()

    def core_add(t, g):
        core_copy(t, g).wait_recv()
        here = pl.ds(pl.multiple_of((2 * g + core) * GROUP, GROUP), GROUP)
        total = acc[t, here, :] + crecv[t, g]
        crecv[t, g] = total
        place, low = g // 2, g % 2
        send1[t, 0, place, low * GROUP : (low + 1) * GROUP, :] = total[:, LEFT].astype(BF16)
        for high in range(2):
            send1[t, 1, high * 2 + low, place * HALF : (place + 1) * HALF, :] = total[
                high * HALF : (high + 1) * HALF, RIGHT
            ].astype(BF16)

    def start1(t):
        for k in (2, 1, 3):
            for color in range(2):
                wide_copy(t, color, 0, k).start()

    def start2(t):
        for color in range(2):
            for k in (1, 2, 3):
                wide_copy(t, color, 0, k).wait_recv()
        for low in range(2):
            for high in range(2):
                rows = slice(low * GROUP + high * HALF, low * GROUP + (high + 1) * HALF)
                total = crecv[t, 2 * x + low, high * HALF : (high + 1) * HALF, LEFT]
                for k in range(3):
                    total = total + recv1[t, 0, k, rows, :].astype(F32)
                own1[t, 0, high * 2 + low] = total
                send2[t, 0, high * 2 + low] = total.astype(BF16)
        for place in range(4):
            rows = slice(place * HALF, (place + 1) * HALF)
            total = crecv[t, 2 * place + y_lo, pl.ds(pl.multiple_of(y_hi * HALF, HALF), HALF), RIGHT]
            for k in range(3):
                total = total + recv1[t, 1, k, rows, :].astype(F32)
            own1[t, 1, place] = total
            send2[t, 1, place] = total.astype(BF16)
        for k in (2, 1, 3):
            for color in range(2):
                wide_copy(t, color, 1, k).start()

    def start3(t):
        for color, mine in ((0, y), (1, x)):
            for k in (1, 2, 3):
                wide_copy(t, color, 1, k).wait_recv()
            total = own1[t, color, mine]
            for k in range(3):
                total = total + recv2[t, color, k].astype(F32)
            own2[t, color] = total
            lanes = (LEFT, RIGHT)[color]
            for part in range(4):
                piece = own2[t, color, part * PIECE : part * PIECE + PIECE, :]
                own3[t, part, :, lanes] = piece
                send3[t, part, :, lanes] = piece.astype(BF16)
        for k in (2, 1, 3):
            last_copy(t, k).start()

    def finish(t, result):
        for k in (1, 2, 3):
            last_copy(t, k).wait_recv()
        total = own3[t, z]
        for k in range(3):
            total = total + recv3[t, k].astype(F32)
        total = total * scale
        result[pl.ds(0, PIECE, stride=2), :] = total[:, LEFT]
        result[pl.ds(1, PIECE, stride=2), :] = total[:, RIGHT]

    def out_copy(r):
        return pltpu.make_async_copy(stage[r], out.at[0, r - 1], out_sem.at[r - 1])

    def last(*rows):
        def keep(total):
            for k, r in enumerate(rows):
                stage[r][...] = (gv[r][...].astype(F32) + total[span(k), :] * slope[r][...]).astype(BF16)
                out_copy(r).start()

        return conv(h3, lambda a, b: wt1[a, b * CHANS : (b + 1) * CHANS, :], rows, True, keep)

    for r in range(4):
        loads[r][1].wait()
    weave(cots(1, 2, 3, 4))
    weights[1].wait()
    for r in range(4):
        loads[r][0].wait()
    pl.semaphore_wait(barrier, len(peers))

    @pl.when(row < 7)
    def _():
        for copy in halos_down:
            copy.start()

    @pl.when(row > 0)
    def _():
        for copy in halos_up:
            copy.start()

    weave(turn(wv2, wt2), acted(1))
    weave(both(backward(2), backward(3)), acted(2, 3, 4))
    weights[0].wait()
    for pair in loads[4:]:
        for copy in pair:
            copy.wait()
    weave(both(forward(2), forward(3)), cots(5, 6, 7, 8) + acted(5, 6))
    weave(both(forward(4, 5), backward(4, 5)), acted(7, 8) + elem(2))
    weave(both(forward(6, 7), backward(6, 7)), elem(3, 4, 5), turn(wv1, wt1))
    weave(one_grads(True, (2, 3), (4, 5)), elem(6, 7))

    @pl.when(row > 0)
    def _():
        for copy in halos_down:
            copy.wait_recv()

    @pl.when(row == 0)
    def _():
        fv[0][...] = jnp.zeros((COLS, CHANS), BF16)
        gv[0][...] = jnp.zeros((COLS, CHANS), BF16)

    @pl.when(row < 7)
    def _():
        for copy in halos_up:
            copy.wait_recv()

    @pl.when(row == 7)
    def _():
        fv[ROWS + 1][...] = jnp.zeros((COLS, CHANS), BF16)
        gv[ROWS + 1][...] = jnp.zeros((COLS, CHANS), BF16)

    weave(one_grads(False, (6, 7)), cots(0, ROWS + 1) + acted(0, ROWS + 1))
    weave(both(forward(1, ROWS), backward(1, ROWS)))
    weave(two_grads(True, (4, 5)), elem(1, ROWS))
    hsend[0] = h3[1][:, CHANS : 2 * CHANS]
    hsend[1] = h3[ROWS][:, CHANS : 2 * CHANS]

    @pl.when(row < 7)
    def _():
        h_down.start()

    @pl.when(row > 0)
    def _():
        h_up.start()

    weave(one_grads(False, (1, ROWS)))
    core_start(0, range(8))
    inner = two_grads(False, (2, 3), (6, 7))
    weave(inner[:4])
    weave(inner[4:], [functools.partial(core_add, 0, g) for g in range(8)])
    start1(0)
    weave(two_edge(0, (ROWS - 1, ROWS), (ROWS, ROWS + 1)))
    core_start(1, (0, 1))
    weave(two_edge(1, (1, ROWS), (1, ROWS)))
    core_start(1, (2, 3, 4))
    weave(two_edge(2, (2, 1), (1, 0)))
    core_start(1, (5, 6, 7))
    inner = both(last(2, 3), last(4, 5))
    weave(inner[:5], [functools.partial(core_add, 1, g) for g in range(5)])
    for g in (5, 6, 7):
        core_add(1, g)
    start1(1)
    weave(inner[5:8], grade(2, 3, 4, 5))
    weave(inner[8:])

    @pl.when(row > 0)
    def _():
        h_down.wait_recv()

    @pl.when(row == 0)
    def _():
        hrecv[0] = jnp.zeros((COLS, CHANS), BF16)

    @pl.when(row < 7)
    def _():
        h_up.wait_recv()

    @pl.when(row == 7)
    def _():
        hrecv[1] = jnp.zeros((COLS, CHANS), BF16)

    weave(single(halo_one, 0, ROWS + 1))
    inner = both(last(6, 7), last(1, ROWS))
    weave(inner[:8], grade(6, 7, 1, ROWS))
    weave(inner[8:])
    start2(0)
    start2(1)
    start3(0)
    start3(1)
    finish(0, out_one)
    finish(1, out_two)

    @pl.when(row < 7)
    def _():
        for copy in halos_down + [h_down]:
            copy.wait_send()

    @pl.when(row > 0)
    def _():
        for copy in halos_up + [h_up]:
            copy.wait_send()

    for r in range(ROWS):
        out_copy(r + 1).wait()
    for t in range(2):
        for g in range(8):
            core_copy(t, g).wait_send()
        for k in (1, 2, 3):
            for color in range(2):
                for step in range(2):
                    wide_copy(t, color, step, k).wait_send()
            last_copy(t, k).wait_send()


def shards(features, cotangent, weight_one, weight_two):
    height = features.shape[1] * lax.axis_size("row")
    scale = 1.0 / math.sqrt(lax.axis_size("img") * height * features.shape[2])
    hbm = pl.BlockSpec(memory_space=pl.ANY)
    vmem = pl.BlockSpec(memory_space=pltpu.VMEM)
    dma = pltpu.SemaphoreType.DMA
    wide = ROWS + 2
    grad, one, two = pl.pallas_call(
        functools.partial(kernel, scale),
        out_shape=(
            jax.ShapeDtypeStruct(features.shape, BF16),
            jax.ShapeDtypeStruct((2 * PIECE, 128), F32),
            jax.ShapeDtypeStruct((2 * PIECE, 128), F32),
        ),
        in_specs=[hbm] * 4,
        out_specs=(hbm, vmem, vmem),
        scratch_shapes=[
            [pltpu.VMEM((COLS, CHANS), BF16)] * wide,
            [pltpu.VMEM((COLS, CHANS), BF16)] * wide,
            pltpu.VMEM((3, 3, CHANS, CHANS), BF16),
            pltpu.VMEM((3, 3, CHANS, CHANS), BF16),
            pltpu.VMEM((3, WIDE, CHANS), BF16),
            pltpu.VMEM((3, WIDE, CHANS), BF16),
            [pltpu.VMEM((COLS, WIDE), BF16)] * wide,
            [pltpu.VMEM((COLS, WIDE), BF16)] * wide,
            [pltpu.VMEM((COLS, WIDE), BF16)] * wide,
            [pltpu.VMEM((CHANS, COLS), BF16)] * wide,
            [pltpu.VMEM((CHANS, COLS), BF16)] * wide,
            [pltpu.VMEM((COLS, CHANS), F32)] * wide,
            [pltpu.VMEM((COLS, CHANS), F32)] * wide,
            [pltpu.VMEM((COLS, CHANS), F32)] * wide,
            pltpu.VMEM((2, COLS, CHANS), BF16),
            pltpu.VMEM((2, COLS, CHANS), BF16),
            [pltpu.VMEM((COLS, CHANS), BF16)] * wide,
            pltpu.VMEM((2, 9 * CHANS, CHANS), F32),
            pltpu.VMEM((2, 8, GROUP, CHANS), F32),
            pltpu.VMEM((2, 2, 4, 2 * GROUP, 128), BF16),
            pltpu.VMEM((2, 2, 3, 2 * GROUP, 128), BF16),
            pltpu.VMEM((2, 2, 4, GROUP // 2, 128), F32),
            pltpu.VMEM((2, 2, 4, GROUP // 2, 128), BF16),
            pltpu.VMEM((2, 2, 3, GROUP // 2, 128), BF16),
            pltpu.VMEM((2, 2, GROUP // 2, 128), F32),
            pltpu.VMEM((2, 4, PIECE, CHANS), BF16),
            pltpu.VMEM((2, 3, PIECE, CHANS), BF16),
            pltpu.VMEM((2, 4, PIECE, CHANS), F32),
            dma((2, ROWS)),
            dma((2,)),
            dma((3, 2)),
            dma((3, 2)),
            dma((ROWS,)),
            dma((2, 8)),
            dma((2, 8)),
            dma((2, 2, 2, 3)),
            dma((2, 2, 2, 3)),
            dma((2, 3)),
            dma((2, 3)),
        ],
        compiler_params=pltpu.CompilerParams(
            collective_id=0, has_side_effects=True, vmem_limit_bytes=64 * 1000 * 1000
        ),
        name="unit_backward",
    )(features, cotangent, weight_one, weight_two)
    return grad, one.reshape(-1), two.reshape(-1)


def solution(mesh):
    placed = (P("img", "row", None, None), P("img", "row", None, None), P(), P())
    return jax.shard_map(
        shards,
        mesh=mesh,
        in_specs=placed,
        out_specs=(P("img", "row", None, None), P(("img", "row")), P(("img", "row"))),
        check_vma=False,
    )
```

```python
import functools
import math

import jax
import jax.numpy as jnp
from jax import lax
from jax.experimental import pallas as pl
from jax.experimental.pallas import tpu as pltpu
from jax.sharding import PartitionSpec as P

MESH = pl.DeviceIdType.MESH
F32 = jnp.float32
BF16 = jnp.bfloat16
COEFF = 0.7978845608028654
CUBIC = 0.044715
ROWS = 8
COLS = 384
CHANS = 256
WIDE = 3 * CHANS
CELLS = ROWS * COLS
GROUP = 144
PIECE = 18


def gelu_terms(v):
    poly = COEFF + (COEFF * CUBIC) * (v * v)
    half = 0.5 + 0.5 * jnp.tanh(v * poly)
    return v * half, half, poly


def slope_of(acted, half, poly):
    return half + acted * (1.0 - half) * (6.0 * poly - 4.0 * COEFF)


def span(row, count=1):
    return slice(row * COLS, (row + count) * COLS)


def rows_of(refs, rows, columns):
    return jnp.concatenate([refs[r][:, columns] for r in rows], axis=0)


def lanes_of(refs, rows):
    return jnp.concatenate([refs[r][...] for r in rows], axis=1)


def weave(*streams):
    longest = max(len(stream) for stream in streams)
    done = [0] * len(streams)
    for step in range(longest):
        for k, stream in enumerate(streams):
            end = (step + 1) * len(stream) // longest
            for task in stream[done[k] : end]:
                task()
            done[k] = end


def kernel(
    scale,
    feat,
    cot,
    w_one,
    w_two,
    out,
    out_one,
    out_two,
    fv,
    gv,
    wv1,
    wv2,
    wt1,
    wt2,
    a3,
    g3,
    h3,
    at,
    gt,
    slope,
    hid,
    bh,
    hsend,
    hrecv,
    stage,
    acc,
    crecv,
    send1,
    recv1,
    own1,
    send2,
    recv2,
    own2,
    send3,
    recv3,
    own3,
    load_sem,
    w_sem,
    halo_send,
    halo_recv,
    out_sem,
    core_send,
    core_recv,
    wide_send,
    wide_recv,
    last_send,
    last_recv,
):
    img, row = lax.axis_index("img"), lax.axis_index("row")
    core, y_lo, x = img % 2, (img // 2) % 2, img // 4
    z, y_hi = row % 4, row // 4
    y = y_hi * 2 + y_lo

    def x_peer(k):
        there = (x + k) % 4
        return there, ((there * 2 + y_lo) * 2 + core, row)

    def y_peer(k):
        there = (y + k) % 4
        return there, ((x * 2 + there % 2) * 2 + core, (there // 2) * 4 + z)

    def z_peer(k):
        there = (z + k) % 4
        return there, (img, y_hi * 4 + there)

    partner = ((x * 2 + y_lo) * 2 + (1 - core), row)
    below, above = (img, (row + 1) % 8), (img, (row + 7) % 8)

    loads = [
        (
            pltpu.make_async_copy(feat.at[0, r], fv[r + 1], load_sem.at[0, r]),
            pltpu.make_async_copy(cot.at[0, r], gv[r + 1], load_sem.at[1, r]),
        )
        for r in range(ROWS)
    ]
    weights = [
        pltpu.make_async_copy(w_one, wv1, w_sem.at[0]),
        pltpu.make_async_copy(w_two, wv2, w_sem.at[1]),
    ]
    for r in range(4):
        loads[r][1].start()
    weights[1].start()
    for r in range(4):
        loads[r][0].start()
    weights[0].start()
    for pair in loads[4:]:
        for copy in reversed(pair):
            copy.start()

    barrier = pltpu.get_barrier_semaphore()
    peers = [partner, below, above]
    for peer in (x_peer, y_peer, z_peer):
        for k in (1, 2, 3):
            peers.append(peer(k)[1])
    for peer in peers:
        pl.semaphore_signal(barrier, inc=1, device_id=peer, device_id_type=MESH)

    def halo(which, down, src, dst):
        return pltpu.make_async_remote_copy(
            src_ref=src,
            dst_ref=dst,
            send_sem=halo_send.at[which, down],
            recv_sem=halo_recv.at[which, down],
            device_id=below if down else above,
            device_id_type=MESH,
        )

    halos_down = [
        halo(0, 1, feat.at[0, ROWS - 1], fv[0]),
        halo(1, 1, cot.at[0, ROWS - 1], gv[0]),
    ]
    halos_up = [
        halo(0, 0, feat.at[0, 0], fv[ROWS + 1]),
        halo(1, 0, cot.at[0, 0], gv[ROWS + 1]),
    ]
    h_down = halo(2, 1, hsend.at[1], hrecv.at[0])
    h_up = halo(2, 0, hsend.at[0], hrecv.at[1])

    def turn(source, target):
        def block(a, b):
            target[a, b * CHANS : (b + 1) * CHANS, :] = source[a, b].T

        return [functools.partial(block, a, b) for a in range(3) for b in range(3)]

    def window(ref, lane, c):
        blank = jnp.zeros((8, 128), F32)
        low, high = 128 * c - 8, 128 * c + 136
        inside = ref[max(low, 0) : min(high, COLS), lane : lane + 128].astype(F32)
        if c == 0:
            inside = jnp.concatenate([blank, inside], axis=0)
        if c == 2:
            inside = jnp.concatenate([inside, blank], axis=0)
        return pltpu.roll(inside, 1, 0)[8:136], pltpu.roll(inside, 143, 0)[8:136]

    def block(lane, c):
        return slice(128 * c, 128 * c + 128), slice(lane, lane + 128)

    def wide_block(lane, c, tap):
        return slice(128 * c, 128 * c + 128), slice(tap * CHANS + lane, tap * CHANS + lane + 128)

    def acted_one(r, lane, c):
        acted, _, _ = gelu_terms(fv[r][block(lane, c)].astype(F32))
        mid = acted.astype(BF16)
        hid[r][block(lane, c)] = acted
        a3[r][wide_block(lane, c, 1)] = mid
        at[r][lane : lane + 128, 128 * c : 128 * c + 128] = mid.T

    def acted_two(r, lane, c):
        left, right = window(hid[r], lane, c)
        a3[r][wide_block(lane, c, 0)] = left.astype(BF16)
        a3[r][wide_block(lane, c, 2)] = right.astype(BF16)

    def cot_one(r, lane, c):
        left, right = window(gv[r], lane, c)
        g3[r][wide_block(lane, c, 0)] = right.astype(BF16)
        g3[r][wide_block(lane, c, 1)] = gv[r][block(lane, c)]
        g3[r][wide_block(lane, c, 2)] = left.astype(BF16)

    def grade_one(r, lane, c):
        slope[r][block(lane, c)] = slope_of(*gelu_terms(fv[r][block(lane, c)].astype(F32)))

    def elem_one(r, lane, c):
        terms = gelu_terms(hid[r][block(lane, c)])
        gt[r][lane : lane + 128, 128 * c : 128 * c + 128] = terms[0].astype(BF16).T
        grad = bh[r][block(lane, c)] * slope_of(*terms)
        bh[r][block(lane, c)] = grad
        h3[r][wide_block(lane, c, 1)] = grad.astype(BF16)

    def elem_two(r, lane, c):
        left, right = window(bh[r], lane, c)
        h3[r][wide_block(lane, c, 0)] = right.astype(BF16)
        h3[r][wide_block(lane, c, 2)] = left.astype(BF16)

    def halo_one(r, lane, c):
        left, right = window(hrecv.at[r // ROWS], lane, c)
        h3[r][wide_block(lane, c, 0)] = right.astype(BF16)
        h3[r][wide_block(lane, c, 1)] = hrecv[r // ROWS, 128 * c : 128 * c + 128, lane : lane + 128]
        h3[r][wide_block(lane, c, 2)] = left.astype(BF16)

    def single(task, *rows):
        return [functools.partial(task, r, lane, c) for r in rows for lane in (0, 128) for c in range(3)]

    def double(one, two, *rows):
        order = ((one, 0), (one, 1), (two, 0), (one, 2), (two, 1), (two, 2))
        return [functools.partial(f, r, lane, c) for r in rows for lane in (0, 128) for f, c in order]

    def acted(*rows):
        return double(acted_one, acted_two, *rows)

    def elem(*rows):
        return double(elem_one, elem_two, *rows)

    def cots(*rows):
        return single(cot_one, *rows)

    def grade(*rows):
        return single(grade_one, *rows)

    def both(*streams):
        def step(tasks):
            for task in tasks:
                task()

        return [functools.partial(step, tasks) for tasks in zip(*streams, strict=True)]

    def conv(source, weight, rows, flip, keep):
        box = [None]

        def step(a, b):
            near = [r - a + 1 if flip else r + a - 1 for r in rows]
            columns = slice(b * CHANS, (b + 1) * CHANS)
            part = jnp.dot(rows_of(source, near, columns), weight(a, b), preferred_element_type=F32)
            box[0] = part if box[0] is None else box[0] + part
            if (a, b) == (2, 2):
                keep(box[0])

        return [functools.partial(step, a, b) for a in range(3) for b in range(3)]

    def keep_in(refs, rows):
        def keep(total):
            for k, r in enumerate(rows):
                refs[r][...] = total[span(k), :]

        return keep

    def forward(*rows):
        return conv(a3, lambda a, b: wv1[a, b], rows, False, keep_in(hid, rows))

    def backward(*rows):
        return conv(
            g3, lambda a, b: wt2[a, b * CHANS : (b + 1) * CHANS, :], rows, True, keep_in(bh, rows)
        )

    def grads(t, fresh, terms, taps=(0, 1, 2)):
        tall = len(taps) * CHANS

        def build(b, low, high):
            box = [None]

            def step(pair, part, final):
                lhs = jnp.concatenate([lanes_of(*pair[k]) for k in range(len(taps))], axis=0)[low:high]
                rhs = rows_of(pair[-1][0], pair[-1][1], slice(b * CHANS, (b + 1) * CHANS))
                deep = slice(part * CHANS, (part + 1) * CHANS)
                product = jnp.dot(lhs[:, deep], rhs[deep, :], preferred_element_type=F32)
                box[0] = product if box[0] is None else box[0] + product
                if final:
                    for k, a in enumerate(taps):
                        start, end = max(low, k * CHANS), min(high, (k + 1) * CHANS)
                        if start < end:
                            base = (a * 3 + b) * CHANS - k * CHANS
                            here = slice(base + start, base + end)
                            piece = box[0][start - low : end - low, :]
                            acc[t, here, :] = piece if fresh else acc[t, here, :] + piece

            return [
                functools.partial(step, pair, part, pair is terms[-1] and part == 2)
                for pair in terms
                for part in range(3)
            ]

        half = tall // 2
        return both(build(0, 0, tall), build(1, 0, tall)) + both(build(2, 0, half), build(2, half, tall))

    def one_grads(fresh, *pairs):
        terms = [[(at, (p + a - 1, q + a - 1)) for a in range(3)] + [(h3, (p, q))] for p, q in pairs]
        return grads(0, fresh, terms)

    def two_grads(fresh, *pairs):
        terms = [[(gt, (p + a - 1, q + a - 1)) for a in range(3)] + [(g3, (p, q))] for p, q in pairs]
        return grads(1, fresh, terms)

    def two_edge(a, left, right):
        return grads(1, False, [[(gt, left), (g3, right)]], (a,))

    def core_copy(t, g):
        return pltpu.make_async_remote_copy(
            src_ref=acc.at[t, pl.ds(pl.multiple_of((2 * g + 1 - core) * GROUP, GROUP), GROUP)],
            dst_ref=crecv.at[t, g],
            send_sem=core_send.at[t, g],
            recv_sem=core_recv.at[t, g],
            device_id=partner,
            device_id_type=MESH,
        )

    def wide_copy(t, color, step, k):
        send, recv = ((send1, recv1), (send2, recv2))[step]
        there, device = (x_peer if color == step else y_peer)(k)
        return pltpu.make_async_remote_copy(
            src_ref=send.at[t, color, there],
            dst_ref=recv.at[t, color, k - 1],
            send_sem=wide_send.at[t, color, step, k - 1],
            recv_sem=wide_recv.at[t, color, step, k - 1],
            device_id=device,
            device_id_type=MESH,
        )

    def last_copy(t, k):
        there, device = z_peer(k)
        return pltpu.make_async_remote_copy(
            src_ref=send3.at[t, there],
            dst_ref=recv3.at[t, k - 1],
            send_sem=last_send.at[t, k - 1],
            recv_sem=last_recv.at[t, k - 1],
            device_id=device,
            device_id_type=MESH,
        )

    HALF = GROUP // 2
    LEFT, RIGHT = slice(0, 128), slice(128, 256)

    def core_start(t, groups):
        for g in groups:
            core_copy(t, g).start()

    def core_add(t, g):
        core_copy(t, g).wait_recv()
        here = pl.ds(pl.multiple_of((2 * g + core) * GROUP, GROUP), GROUP)
        total = acc[t, here, :] + crecv[t, g]
        crecv[t, g] = total
        place, low = g // 2, g % 2
        send1[t, 0, place, low * GROUP : (low + 1) * GROUP, :] = total[:, LEFT].astype(BF16)
        for high in range(2):
            send1[t, 1, high * 2 + low, place * HALF : (place + 1) * HALF, :] = total[
                high * HALF : (high + 1) * HALF, RIGHT
            ].astype(BF16)

    def start1(t):
        for k in (2, 1, 3):
            for color in range(2):
                wide_copy(t, color, 0, k).start()

    def start2(t):
        for color in range(2):
            for k in (1, 2, 3):
                wide_copy(t, color, 0, k).wait_recv()
        for low in range(2):
            for high in range(2):
                rows = slice(low * GROUP + high * HALF, low * GROUP + (high + 1) * HALF)
                total = crecv[t, 2 * x + low, high * HALF : (high + 1) * HALF, LEFT]
                for k in range(3):
                    total = total + recv1[t, 0, k, rows, :].astype(F32)
                own1[t, 0, high * 2 + low] = total
                send2[t, 0, high * 2 + low] = total.astype(BF16)
        for place in range(4):
            rows = slice(place * HALF, (place + 1) * HALF)
            total = crecv[t, 2 * place + y_lo, pl.ds(pl.multiple_of(y_hi * HALF, HALF), HALF), RIGHT]
            for k in range(3):
                total = total + recv1[t, 1, k, rows, :].astype(F32)
            own1[t, 1, place] = total
            send2[t, 1, place] = total.astype(BF16)
        for k in (2, 1, 3):
            for color in range(2):
                wide_copy(t, color, 1, k).start()

    def start3(t):
        for color, mine in ((0, y), (1, x)):
            for k in (1, 2, 3):
                wide_copy(t, color, 1, k).wait_recv()
            total = own1[t, color, mine]
            for k in range(3):
                total = total + recv2[t, color, k].astype(F32)
            own2[t, color] = total
            lanes = (LEFT, RIGHT)[color]
            for part in range(4):
                piece = own2[t, color, part * PIECE : part * PIECE + PIECE, :]
                own3[t, part, :, lanes] = piece
                send3[t, part, :, lanes] = piece.astype(BF16)
        for k in (2, 1, 3):
            last_copy(t, k).start()

    def finish(t, result):
        for k in (1, 2, 3):
            last_copy(t, k).wait_recv()
        total = own3[t, z]
        for k in range(3):
            total = total + recv3[t, k].astype(F32)
        total = total * scale
        result[pl.ds(0, PIECE, stride=2), :] = total[:, LEFT]
        result[pl.ds(1, PIECE, stride=2), :] = total[:, RIGHT]

    def out_copy(r):
        return pltpu.make_async_copy(stage[r], out.at[0, r - 1], out_sem.at[r - 1])

    def last(*rows):
        def keep(total):
            for k, r in enumerate(rows):
                stage[r][...] = (gv[r][...].astype(F32) + total[span(k), :] * slope[r][...]).astype(BF16)
                out_copy(r).start()

        return conv(h3, lambda a, b: wt1[a, b * CHANS : (b + 1) * CHANS, :], rows, True, keep)

    for r in range(4):
        loads[r][1].wait()
    weave(cots(1, 2, 3, 4))
    weights[1].wait()
    for r in range(4):
        loads[r][0].wait()
    pl.semaphore_wait(barrier, len(peers))

    @pl.when(row < 7)
    def _():
        for copy in halos_down:
            copy.start()

    @pl.when(row > 0)
    def _():
        for copy in halos_up:
            copy.start()

    weave(turn(wv2, wt2), acted(1))
    weave(both(backward(2), backward(3)), acted(2, 3, 4))
    weights[0].wait()
    for pair in loads[4:]:
        for copy in pair:
            copy.wait()
    weave(both(forward(2), forward(3)), cots(5, 6, 7, 8) + acted(5, 6))
    weave(both(forward(4, 5), backward(4, 5)), acted(7, 8) + elem(2))
    weave(both(forward(6, 7), backward(6, 7)), elem(3, 4, 5), turn(wv1, wt1))
    weave(one_grads(True, (2, 3), (4, 5)), elem(6, 7))

    @pl.when(row > 0)
    def _():
        for copy in halos_down:
            copy.wait_recv()

    @pl.when(row == 0)
    def _():
        fv[0][...] = jnp.zeros((COLS, CHANS), BF16)
        gv[0][...] = jnp.zeros((COLS, CHANS), BF16)

    @pl.when(row < 7)
    def _():
        for copy in halos_up:
            copy.wait_recv()

    @pl.when(row == 7)
    def _():
        fv[ROWS + 1][...] = jnp.zeros((COLS, CHANS), BF16)
        gv[ROWS + 1][...] = jnp.zeros((COLS, CHANS), BF16)

    weave(one_grads(False, (6, 7)), cots(0, ROWS + 1) + acted(0, ROWS + 1))
    weave(both(forward(1, ROWS), backward(1, ROWS)))
    weave(two_grads(True, (4, 5)), elem(1, ROWS))
    hsend[0] = h3[1][:, CHANS : 2 * CHANS]
    hsend[1] = h3[ROWS][:, CHANS : 2 * CHANS]

    @pl.when(row < 7)
    def _():
        h_down.start()

    @pl.when(row > 0)
    def _():
        h_up.start()

    weave(one_grads(False, (1, ROWS)))
    core_start(0, range(8))
    inner = two_grads(False, (2, 3), (6, 7))
    weave(inner[:4])
    weave(inner[4:], [functools.partial(core_add, 0, g) for g in range(8)])
    start1(0)
    weave(two_edge(0, (ROWS - 1, ROWS), (ROWS, ROWS + 1)))
    core_start(1, (0, 1))
    weave(two_edge(1, (1, ROWS), (1, ROWS)))
    core_start(1, (2, 3, 4))
    weave(two_edge(2, (2, 1), (1, 0)))
    core_start(1, (5, 6, 7))
    inner = both(last(2, 3), last(4, 5))
    weave(inner[:5], [functools.partial(core_add, 1, g) for g in range(5)])
    for g in (5, 6, 7):
        core_add(1, g)
    start1(1)
    weave(inner[5:8], grade(2, 3, 4, 5))
    weave(inner[8:])

    @pl.when(row > 0)
    def _():
        h_down.wait_recv()

    @pl.when(row == 0)
    def _():
        hrecv[0] = jnp.zeros((COLS, CHANS), BF16)

    @pl.when(row < 7)
    def _():
        h_up.wait_recv()

    @pl.when(row == 7)
    def _():
        hrecv[1] = jnp.zeros((COLS, CHANS), BF16)

    weave(single(halo_one, 0, ROWS + 1))
    inner = both(last(6, 7), last(1, ROWS))
    weave(inner[:8], grade(6, 7, 1, ROWS))
    weave(inner[8:])
    start2(0)
    start2(1)
    start3(0)
    start3(1)
    finish(0, out_one)
    finish(1, out_two)

    @pl.when(row < 7)
    def _():
        for copy in halos_down + [h_down]:
            copy.wait_send()

    @pl.when(row > 0)
    def _():
        for copy in halos_up + [h_up]:
            copy.wait_send()

    for r in range(ROWS):
        out_copy(r + 1).wait()
    for t in range(2):
        for g in range(8):
            core_copy(t, g).wait_send()
        for k in (1, 2, 3):
            for color in range(2):
                for step in range(2):
                    wide_copy(t, color, step, k).wait_send()
            last_copy(t, k).wait_send()


def hand_over(grad, one, two, out, out_one, out_two, rows, small, in_sem, out_sem):
    places = [(grad.at[0, r], rows[r], out.at[0, r]) for r in range(ROWS)]
    places += [(one, small[0], out_one), (two, small[1], out_two)]
    ins = [pltpu.make_async_copy(src, mid, in_sem.at[k]) for k, (src, mid, _) in enumerate(places)]
    outs = [pltpu.make_async_copy(mid, dst, out_sem.at[k]) for k, (_, mid, dst) in enumerate(places)]
    for copy in ins:
        copy.start()
    for before, after in zip(ins, outs, strict=True):
        before.wait()
        after.start()
    for copy in outs:
        copy.wait()


def shards(features, cotangent, weight_one, weight_two):
    height = features.shape[1] * lax.axis_size("row")
    scale = 1.0 / math.sqrt(lax.axis_size("img") * height * features.shape[2])
    hbm = pl.BlockSpec(memory_space=pl.ANY)
    vmem = pl.BlockSpec(memory_space=pltpu.VMEM)
    dma = pltpu.SemaphoreType.DMA
    wide = ROWS + 2
    grad, one, two = pl.pallas_call(
        functools.partial(kernel, scale),
        out_shape=(
            jax.ShapeDtypeStruct(features.shape, BF16),
            jax.ShapeDtypeStruct((2 * PIECE, 128), F32),
            jax.ShapeDtypeStruct((2 * PIECE, 128), F32),
        ),
        in_specs=[hbm] * 4,
        out_specs=(hbm, vmem, vmem),
        scratch_shapes=[
            [pltpu.VMEM((COLS, CHANS), BF16)] * wide,
            [pltpu.VMEM((COLS, CHANS), BF16)] * wide,
            pltpu.VMEM((3, 3, CHANS, CHANS), BF16),
            pltpu.VMEM((3, 3, CHANS, CHANS), BF16),
            pltpu.VMEM((3, WIDE, CHANS), BF16),
            pltpu.VMEM((3, WIDE, CHANS), BF16),
            [pltpu.VMEM((COLS, WIDE), BF16)] * wide,
            [pltpu.VMEM((COLS, WIDE), BF16)] * wide,
            [pltpu.VMEM((COLS, WIDE), BF16)] * wide,
            [pltpu.VMEM((CHANS, COLS), BF16)] * wide,
            [pltpu.VMEM((CHANS, COLS), BF16)] * wide,
            [pltpu.VMEM((COLS, CHANS), F32)] * wide,
            [pltpu.VMEM((COLS, CHANS), F32)] * wide,
            [pltpu.VMEM((COLS, CHANS), F32)] * wide,
            pltpu.VMEM((2, COLS, CHANS), BF16),
            pltpu.VMEM((2, COLS, CHANS), BF16),
            [pltpu.VMEM((COLS, CHANS), BF16)] * wide,
            pltpu.VMEM((2, 9 * CHANS, CHANS), F32),
            pltpu.VMEM((2, 8, GROUP, CHANS), F32),
            pltpu.VMEM((2, 2, 4, 2 * GROUP, 128), BF16),
            pltpu.VMEM((2, 2, 3, 2 * GROUP, 128), BF16),
            pltpu.VMEM((2, 2, 4, GROUP // 2, 128), F32),
            pltpu.VMEM((2, 2, 4, GROUP // 2, 128), BF16),
            pltpu.VMEM((2, 2, 3, GROUP // 2, 128), BF16),
            pltpu.VMEM((2, 2, GROUP // 2, 128), F32),
            pltpu.VMEM((2, 4, PIECE, CHANS), BF16),
            pltpu.VMEM((2, 3, PIECE, CHANS), BF16),
            pltpu.VMEM((2, 4, PIECE, CHANS), F32),
            dma((2, ROWS)),
            dma((2,)),
            dma((3, 2)),
            dma((3, 2)),
            dma((ROWS,)),
            dma((2, 8)),
            dma((2, 8)),
            dma((2, 2, 2, 3)),
            dma((2, 2, 2, 3)),
            dma((2, 3)),
            dma((2, 3)),
        ],
        compiler_params=pltpu.CompilerParams(
            collective_id=0, has_side_effects=True, vmem_limit_bytes=64 * 1000 * 1000
        ),
        name="unit_backward",
    )(features, cotangent, weight_one, weight_two)
    grad, one, two = pl.pallas_call(
        hand_over,
        out_shape=(
            jax.ShapeDtypeStruct(features.shape, BF16),
            jax.ShapeDtypeStruct((2 * PIECE, 128), F32),
            jax.ShapeDtypeStruct((2 * PIECE, 128), F32),
        ),
        in_specs=[hbm] * 3,
        out_specs=(hbm,) * 3,
        scratch_shapes=[
            [pltpu.VMEM((COLS, CHANS), BF16)] * ROWS,
            [pltpu.VMEM((2 * PIECE, 128), F32)] * 2,
            dma((ROWS + 2,)),
            dma((ROWS + 2,)),
        ],
        compiler_params=pltpu.CompilerParams(vmem_limit_bytes=64 * 1000 * 1000),
        name="hand_over",
    )(grad, one, two)
    return grad, one.reshape(-1), two.reshape(-1)


def solution(mesh):
    placed = (P("img", "row", None, None), P("img", "row", None, None), P(), P())
    return jax.shard_map(
        shards,
        mesh=mesh,
        in_specs=placed,
        out_specs=(P("img", "row", None, None), P(("img", "row")), P(("img", "row"))),
        check_vma=False,
    )
```
